256 devices in a mesh: gx: 32 (over x, z), gy: 8 (over y, core).
Axes of the slice: x: 4, y: 4, z: 8, core: 2. Of those that a mesh axis runs over, the one named last changes fastest.
Arguments:
- source: float32 [6, 256, 128, 128], P(None, 'gx', 'gy'), may hold values from -6 to 6
- cell_class: int32 [256, 128, 128], P('gx', 'gy'), may hold values from 0 to 7
- class_conductivity: float32 [8], replicated, may hold values from 0.1 to 3
- layer_of_depth: int32 [64], replicated, may hold values from 0 to 7
- inverses: float32 [8, 192, 192], replicated, as said below
Outputs:
- correction: float32 [6, 256, 128, 128], P(None, 'gx', 'gy')
The draws below stay inside these ranges and needn't reach their ends.
Inputs may be any that keep to these rules, and one draw needn't show every extreme that they name: `inverses`: each matrix has a positive diagonal.
All inputs are finite; a program needn't handle non-finite values.
Results may differ from the reference program's by a relative error of at most 0.000054.
Values sent between devices are 32-bit elements; how exact they have to be, the bound alone decides.
No kernel may reach another device: no remote copies, remote signals or barrier semaphores. Data moves between devices by JAX's collectives and lax.ppermute only.
A program may use at most 128 MiB of HBM per device.

```python
import math
import jax
import jax.numpy as jnp
from jax import lax

CZ = 128
BLOCK = 192
NLAYER = 8
NCLASS = 8
NX = 256
NY = 128
NZB = 64


def draw_inverses(key, part):
    key_diag, key_off = jax.random.split(key, 2)
    diag = jax.random.uniform(key_diag, (NLAYER, BLOCK), jnp.float32, 0.12, 0.2)
    off = jax.random.normal(key_off, (NLAYER, BLOCK, BLOCK), jnp.float32) * 0.008
    eye = jnp.eye(BLOCK, dtype=jnp.float32)
    return off * (1.0 - eye[None]) + eye[None] * diag[:, :, None]


def set_ends(values, own_key, low, high):
    place = [jax.random.randint(jax.random.fold_in(own_key, axis), (), 0, length) for axis, length in enumerate(values.shape)]
    longest = values.shape.index(max(values.shape))
    neighbour = place[:longest] + [(place[longest] + 1) % values.shape[longest]] + place[longest + 1:]
    return values.at[tuple(place)].set(low).at[tuple(neighbour)].set(high)


def level_of(own_key, extent, cuts, smallest, high):
    factor_of = 1.0
    for axis_at, parts in cuts:
        draws = jax.random.uniform(jax.random.fold_in(jax.random.fold_in(own_key, 6), axis_at), (parts,), jnp.float32, smallest / len(cuts), high / len(cuts))
        factor_of = factor_of * jnp.repeat(jnp.exp(draws), extent[axis_at] // parts).reshape((-1,) + (1,) * (len(extent) - 1 - axis_at))
    return factor_of


def gaussian(key, dims, spread, reach, pieces=(), kind=jnp.bfloat16):
    array = jax.random.normal(key, dims, jnp.float32) * spread
    if len(pieces) > 0:
        array = level_of(key, dims, pieces, -0.22, 0.18) * array
    return jnp.clip(array, min=-reach, max=reach).astype(kind)


def setup_inputs(seed: int = 0) -> dict:
    key_list = jax.random.split(jax.random.key(seed), 6)
    source = gaussian(key_list[0], (6, NX, NY, CZ), 1.0, 6.0, ((1, 32), (2, 8)), jnp.float32)
    cell_class = set_ends(jax.random.randint(key_list[1], (NX, NY, CZ), 0, NCLASS), jax.random.fold_in(key_list[1], 1), 0, NCLASS - 1).astype(jnp.int32)
    class_conductivity = jnp.clip(jnp.exp(jax.random.uniform(key_list[2], (NCLASS,), jnp.float32, math.log(0.1), math.log(3.0))), 0.1, 3.0)
    layer_of_depth = set_ends(jax.random.randint(key_list[3], (NZB,), 0, NLAYER), jax.random.fold_in(key_list[3], 1), 0, NLAYER - 1).astype(jnp.int32)
    inverses = draw_inverses(jax.random.fold_in(key_list[5], 71), 0)
    return {"source": source, "cell_class": cell_class, "class_conductivity": class_conductivity, "layer_of_depth": layer_of_depth, "inverses": inverses}


damping = 0.8


def apply_operator(field, sigma, level):
    padded = jnp.pad(field, ((0, 0), (1, 1), (1, 1), (1, 1)))
    beside = padded[:, 2:, 1:-1, 1:-1] + padded[:, :-2, 1:-1, 1:-1]
    beside = beside + padded[:, 1:-1, 2:, 1:-1] + padded[:, 1:-1, :-2, 1:-1]
    beside = beside + padded[:, 1:-1, 1:-1, 2:] + padded[:, 1:-1, 1:-1, :-2]
    lapl = (6.0 * field - beside) / (4.0 ** level)
    real_part = lapl[:3] - sigma[None] * field[3:]
    imag_part = lapl[3:] + sigma[None] * field[:3]
    return jnp.concatenate([real_part, imag_part], axis=0)


def to_blocks(field):
    comps, sx, sy, sz = field.shape
    shaped = field.reshape(comps, sx // 4, 4, sy // 4, 4, sz // 2, 2)
    return shaped.transpose(5, 1, 3, 0, 2, 4, 6).reshape(sz // 2, (sx // 4) * (sy // 4), comps * 32)


def from_blocks(blocks, comps, sx, sy, sz):
    shaped = blocks.reshape(sz // 2, sx // 4, sy // 4, comps, 4, 4, 2)
    return shaped.transpose(3, 1, 4, 2, 5, 0, 6).reshape(comps, sx, sy, sz)


def smooth(field, inverses, layer_ids, level):
    comps, sx, sy, sz = field.shape
    blocks = to_blocks(field)
    matrices = jnp.take(inverses, layer_ids.astype(jnp.int32), axis=0)
    total = jnp.einsum("zrk,zjk->zrj", blocks, matrices, precision=lax.Precision.HIGHEST)
    total = total * (damping * 4.0 ** level)
    return from_blocks(total, comps, sx, sy, sz)


def restrict(field):
    sx, sy, sz = field.shape[-3:]
    shaped = field.reshape(field.shape[:-3] + (sx // 2, 2, sy // 2, 2, sz // 2, 2))
    return shaped.mean(axis=(-5, -3, -1))


def prolong(field):
    return jnp.repeat(jnp.repeat(jnp.repeat(field, 2, axis=-3), 2, axis=-2), 2, axis=-1)


def reference(source, cell_class, class_conductivity, layer_of_depth, inverses):
    sigma0 = jnp.zeros(cell_class.shape, class_conductivity.dtype)
    for index in range(NCLASS):
        sigma0 = sigma0 + jnp.where(cell_class == index, class_conductivity[index], 0.0)
    sigma1 = restrict(sigma0)
    layers0 = layer_of_depth
    layers1 = layer_of_depth[::2]
    rhs0 = source
    x0 = smooth(rhs0, inverses, layers0, 0)
    rhs1 = restrict(rhs0 - apply_operator(x0, sigma0, 0))
    x1 = smooth(rhs1, inverses, layers1, 1)
    x1 = x1 + smooth(rhs1 - apply_operator(x1, sigma1, 1), inverses, layers1, 1)
    x0 = x0 + prolong(x1)
    x0 = x0 + smooth(rhs0 - apply_operator(x0, sigma0, 0), inverses, layers0, 0)
    return x0
```

```python
import jax
import jax.numpy as jnp
from jax import lax
from jax.experimental import pallas as pl
from jax.experimental.pallas import tpu as pltpu
from jax.sharding import PartitionSpec as P

damping = 0.8
F32 = jnp.float32
BF16 = jnp.bfloat16


def lane_of(shape):
    return lax.broadcasted_iota(jnp.int32, shape, 1)


def row_of(shape):
    return lax.broadcasted_iota(jnp.int32, shape, 0)


def take_lanes(v, index):
    return jnp.take_along_axis(v, index, axis=1, mode="promise_in_bounds")


def take_rows(v, index):
    return jnp.take_along_axis(v, index, axis=0, mode="promise_in_bounds")


def split_index(shape):
    j = lane_of(shape)
    return ((j & 63) << 1) | (j >> 6)


def join_index(shape):
    j = lane_of(shape)
    return ((j & 1) << 6) | (j >> 1)


class Blocker:
    def __init__(self, half):
        s = row_of((8, 128))
        j = lane_of((8, 128))
        self.half = half
        self.stay = (s < 4) == ((j & (2 * half - 1)) < half)
        self.to = ((s & 1) << 2) | (s >> 1)
        self.back = ((s & 3) << 1) | (s >> 2)

    def swap(self, v):
        return jnp.where(self.stay, v, pltpu.roll(pltpu.roll(v, 4, 0), self.half, 1))

    def forward(self, v):
        return take_rows(self.swap(v), self.to)

    def inverse(self, v):
        return self.swap(take_rows(v, self.back))


def dot(a, b):
    return lax.dot_general(a, b, (((1,), (0,)), ((), ())), preferred_element_type=F32)


def block_product(x, high, low, layer):
    x_high = x.astype(BF16)
    x_low = (x - x_high.astype(F32)).astype(BF16)
    total = jnp.zeros(x.shape, F32)
    for index in range(high.shape[0]):
        part = dot(high[index], x_high) + dot(low[index], x_high) + dot(high[index], x_low)
        total = jnp.where(layer == index, part, total)
    return total


def fine_layers(depth_ref):
    v = depth_ref[...]
    return jnp.concatenate([v, v, v, v], axis=1)


def coarse_layers(depth_ref):
    v = depth_ref[...]
    v = jnp.broadcast_to(jnp.concatenate([v, v], axis=1), (8, 128))
    return take_lanes(v, (lane_of((8, 128)) & 31) << 1)[0:1]


def fine_columns(blocker, get, put):
    for c in range(6):
        for x in range(8):
            v = get(c, x)
            for t in range(2):
                put(c * 32 + (x % 4) * 8, ((x // 4) * 2 + t) * 128, blocker.forward(v[8 * t : 8 * t + 8]))


def fine_smooth(blocker, columns, high, low, layer, put):
    for bx in range(2):
        total = block_product(columns[:, bx * 256 : bx * 256 + 256], high, low, layer) * damping
        for c in range(6):
            for x in range(4):
                row = c * 32 + x * 8
                for t in range(2):
                    put(c, 4 * bx + x, t, blocker.inverse(total[row : row + 8, 128 * t : 128 * t + 128]))


def store_columns(columns):
    def put(row, lane, v):
        columns[row : row + 8, lane : lane + 128] = v

    return put


def coarse_smooth(blocker, columns, get, high, low, layer):
    for c in range(6):
        for x in range(4):
            row = c * 32 + x * 8
            columns[row : row + 8, :] = blocker.forward(get(c, x))
    total = block_product(columns[...], high, low, layer) * (damping * 4.0)
    return lambda c, x: blocker.inverse(total[c * 32 + x * 8 : c * 32 + x * 8 + 8])


def first_kernel(source, depth, inverses, x0, high, low, x_first, x_last, y_first, y_last, columns):
    blocker = Blocker(64)
    for index in range(8):
        m = inverses[index]
        m_high = m.astype(BF16)
        high[index] = m_high
        low[index] = (m - m_high.astype(F32)).astype(BF16)
    split = split_index((16, 128))
    fine_columns(blocker, lambda c, x: take_lanes(source[c, x], split), store_columns(columns))

    def put(c, x, t, v):
        x0[c, x, 8 * t : 8 * t + 8, :] = v
        if x == 0:
            x_first[c, 8 * t : 8 * t + 8, :] = v
        if x == 7:
            x_last[c, 8 * t : 8 * t + 8, :] = v
        if t == 0:
            y_first[c, x : x + 1, :] = v[0:1]
        if t == 1:
            y_last[c, x : x + 1, :] = v[7:8]

    fine_smooth(blocker, columns, high, low, fine_layers(depth), put)


def around(u, y_before, y_after, half, other, keep, row):
    size = u.shape[0]
    before = jnp.where(row == 0, y_before, pltpu.roll(u, 1, 0))
    after = jnp.where(row == size - 1, y_after, pltpu.roll(u, size - 1, 0))
    return before + after + pltpu.roll(u, half, 1) + jnp.where(keep, take_lanes(u, other), 0.0)


def fine_other(shape):
    j = lane_of(shape)
    return jnp.where(j < 64, jnp.maximum(j + 63, 64), jnp.minimum(j - 63, 63)), (j != 0) & (j != 127)


def coarse_other(shape):
    j = lane_of(shape) & 63
    return jnp.where(j < 32, jnp.maximum(j + 31, 32), jnp.minimum(j - 31, 31)), (j != 0) & (j != 63)


def second_kernel(
    conductivity, source, classes, depth, x0, x_before, x_after, y_before, y_after, high, low,
    r0, b1, x1, sigma0, sigma1, x_first, x_last, y_first, y_last, rows, columns,
):
    shape = (16, 128)
    split = split_index(shape)
    other, keep = fine_other(shape)
    row = row_of(shape)
    j = lane_of(shape)
    pair = ((j & 31) << 1) | ((j >> 5) & 1)

    def restrict(v, slot):
        rows[slot] = take_lanes(v + pltpu.roll(v, 64, 1), pair)
        return (rows[slot, pl.ds(0, 8, stride=2), :] + rows[slot, pl.ds(1, 8, stride=2), :]) * 0.125

    for xx in range(4):
        sums = [None] * 7
        for x in (2 * xx, 2 * xx + 1):
            kind = take_lanes(classes[x], split)
            sigma = jnp.zeros(shape, F32)
            for index in range(8):
                sigma = jnp.where(kind == index, conductivity[index], sigma)
            sigma0[x] = sigma
            for c in range(3):
                re = x0[c, x]
                im = x0[c + 3, x]
                for comp, u, turn in ((c, re, -im), (c + 3, im, re)):
                    beside = around(
                        u, y_before[comp, x : x + 1], y_after[comp, x : x + 1], 64, other, keep, row
                    )
                    beside = beside + (x0[comp, x - 1] if x > 0 else x_before[comp])
                    beside = beside + (x0[comp, x + 1] if x < 7 else x_after[comp])
                    rest = take_lanes(source[comp, x], split) - (6.0 * u - beside + sigma * turn)
                    r0[comp, x] = rest
                    sums[comp] = rest if sums[comp] is None else sums[comp] + rest
            sums[6] = sigma if sums[6] is None else sums[6] + sigma
        for c in range(6):
            b1[c, xx] = restrict(sums[c], xx * 7 + c)
        sigma1[xx] = restrict(sums[6], xx * 7 + 6)
    result = coarse_smooth(Blocker(32), columns, lambda c, x: b1[c, x], high, low, coarse_layers(depth))
    store_coarse(result, x1, x_first, x_last, y_first, y_last)


def store_coarse(result, x1, x_first, x_last, y_first, y_last):
    for c in range(6):
        for x in range(4):
            v = result(c, x)
            x1[c, x] = v
            if x == 0:
                x_first[c] = v
            if x == 3:
                x_last[c] = v
            y_first[c, x : x + 1, :] = v[0:1]
            y_last[c, x : x + 1, :] = v[7:8]


def middle_kernel(depth, x0, r0, high, low, y0, columns):
    blocker = Blocker(64)
    fine_columns(blocker, lambda c, x: r0[c, x], store_columns(columns))

    def put(c, x, t, v):
        y0[c, x, 8 * t : 8 * t + 8, :] = x0[c, x, 8 * t : 8 * t + 8, :] + v

    fine_smooth(blocker, columns, high, low, fine_layers(depth), put)


def third_kernel(
    depth, b1, x1a, sigma1, x_before, x_after, y_before, y_after, high, low,
    x1, x_first, x_last, y_first, y_last, columns,
):
    shape = (8, 128)
    other, keep = coarse_other(shape)
    row = row_of(shape)

    def residual(c, x):
        u = x1a[c, x]
        turn = -x1a[c + 3, x] if c < 3 else x1a[c - 3, x]
        beside = around(u, y_before[c, x : x + 1], y_after[c, x : x + 1], 32, other, keep, row)
        beside = beside + (x1a[c, x - 1] if x > 0 else x_before[c])
        beside = beside + (x1a[c, x + 1] if x < 3 else x_after[c])
        return b1[c, x] - ((6.0 * u - beside) * 0.25 + sigma1[x] * turn)

    more = coarse_smooth(Blocker(32), columns, residual, high, low, coarse_layers(depth))
    store_coarse(lambda c, x: x1a[c, x] + more(c, x), x1, x_first, x_last, y_first, y_last)


def last_kernel(
    depth, y0, x1, sigma0, x_before, x_after, y_before, y_after, high, low, out, coarse, image, base, columns
):
    shape = (8, 128)
    j = lane_of(shape)
    row = row_of(shape)
    k = j & 63
    self_index = ((k & 1) << 5) | (k >> 1)
    beyond = jnp.where(j < 64, k - 1, k + 1)
    inside = (beyond >= 0) & (beyond < 64)
    beyond = jnp.clip(beyond, 0, 63)
    next_index = ((beyond & 1) << 5) | (beyond >> 1)

    for c in range(6):
        coarse[c, 0] = take_lanes(x_before[c], self_index)
        coarse[c, 5] = take_lanes(x_after[c], self_index)
        for x in range(4):
            coarse[c, x + 1] = take_lanes(x1[c, x], self_index)
    for xx in range(4):
        for c in range(3):
            own = {}
            for comp in (c, c + 3):
                v = coarse[comp, xx + 1]
                beside = jnp.where(inside, take_lanes(x1[comp, xx], next_index), 0.0)
                low_y = take_lanes(jnp.broadcast_to(y_before[comp, xx : xx + 1], shape), self_index)
                high_y = take_lanes(jnp.broadcast_to(y_after[comp, xx : xx + 1], shape), self_index)
                before = jnp.where(row == 0, low_y, pltpu.roll(v, 1, 0))
                after = jnp.where(row == 7, high_y, pltpu.roll(v, 7, 0))
                own[comp] = (v, 3.0 * v - beside, before, after)
            for half in range(2):
                x = 2 * xx + half
                for parity in range(2):
                    sigma = sigma0[x, pl.ds(parity, 8, stride=2), :]
                    for comp, partner, sign in ((c, c + 3, -1.0), (c + 3, c, 1.0)):
                        v, kept, before, after = own[comp]
                        turned = kept - coarse[comp, xx + 2 * half] - (before, after)[parity]
                        value = turned + sign * sigma * own[partner][0]
                        image[comp, x, pl.ds(parity, 8, stride=2), :] = value
            for comp in (c, c + 3):
                base[comp, xx, pl.ds(0, 8, stride=2), :] = own[comp][0]
                base[comp, xx, pl.ds(1, 8, stride=2), :] = own[comp][0]

    blocker = Blocker(64)
    fine_columns(blocker, lambda c, x: image[c, x], store_columns(columns))
    join = join_index(shape)

    def put(c, x, t, v):
        part = slice(8 * t, 8 * t + 8)
        out[c, x, part, :] = take_lanes(y0[c, x, part, :] + base[c, x // 2, part, :] - v, join)

    fine_smooth(blocker, columns, high, low, fine_layers(depth), put)


def call(kernel, outs, args, scratch, scalars=0):
    vmem = pl.BlockSpec(memory_space=pltpu.VMEM)
    smem = pl.BlockSpec(memory_space=pltpu.SMEM)
    return pl.pallas_call(
        kernel,
        out_shape=[jax.ShapeDtypeStruct(shape, dtype) for shape, dtype in outs],
        in_specs=[smem] * scalars + [vmem] * (len(args) - scalars),
        out_specs=[vmem] * len(outs),
        scratch_shapes=[pltpu.VMEM(shape, F32) for shape in scratch],
        name=kernel.__name__,
    )(*args)


def exchange(x_first, x_last, y_first, y_last):
    def shifted(array, axis, step):
        size = lax.axis_size(axis)
        return lax.ppermute(array, axis, [(i, i + step) for i in range(size) if 0 <= i + step < size])

    return (
        shifted(x_last, "gx", 1),
        shifted(x_first, "gx", -1),
        shifted(y_last, "gy", 1),
        shifted(y_first, "gy", -1),
    )


def per_device(source, cell_class, class_conductivity, layer_of_depth, inverses):
    depth = layer_of_depth.reshape(1, 64)
    fine = ((6, 8, 16, 128), F32)
    coarse = ((6, 4, 8, 128), F32)
    matrices = ((8, 192, 192), BF16)
    fine_faces = [((6, 16, 128), F32)] * 2 + [((6, 8, 128), F32)] * 2
    coarse_faces = [((6, 8, 128), F32)] * 2 + [((6, 4, 128), F32)] * 2

    x0, high, low, *faces = call(
        first_kernel, [fine, matrices, matrices] + fine_faces, (source, depth, inverses), [(192, 512)]
    )
    halos = exchange(*faces)
    r0, b1, x1a, sigma0, sigma1, *faces = call(
        second_kernel,
        [fine, coarse, coarse, ((8, 16, 128), F32), ((4, 8, 128), F32)] + coarse_faces,
        (class_conductivity, source, cell_class, depth, x0, *halos, high, low),
        [(28, 16, 128), (192, 128)],
        scalars=1,
    )
    halos = exchange(*faces)
    (y0,) = call(middle_kernel, [fine], (depth, x0, r0, high, low), [(192, 512)])
    x1, *faces = call(
        third_kernel, [coarse] + coarse_faces, (depth, b1, x1a, sigma1, *halos, high, low), [(192, 128)]
    )
    halos = exchange(*faces)
    (out,) = call(
        last_kernel,
        [fine],
        (depth, y0, x1, sigma0, *halos, high, low),
        [(6, 6, 8, 128), (6, 8, 16, 128), (6, 4, 16, 128), (192, 512)],
    )
    return out


def solution(mesh):
    placed = (P(None, "gx", "gy", None), P("gx", "gy", None), P(), P(), P())
    return jax.shard_map(
        per_device, mesh=mesh, in_specs=placed, out_specs=P(None, "gx", "gy", None), check_vma=False
    )
```

```python
import jax
import jax.numpy as jnp
from jax import lax
from jax.experimental import pallas as pl
from jax.experimental.pallas import tpu as pltpu
from jax.sharding import PartitionSpec as P

damping = 0.8
F32 = jnp.float32
BF16 = jnp.bfloat16


def lane_of(shape):
    return lax.broadcasted_iota(jnp.int32, shape, 1)


def row_of(shape):
    return lax.broadcasted_iota(jnp.int32, shape, 0)


def take_lanes(v, index):
    return jnp.take_along_axis(v, index, axis=1, mode="promise_in_bounds")


def take_rows(v, index):
    return jnp.take_along_axis(v, index, axis=0, mode="promise_in_bounds")


def split_index(shape):
    j = lane_of(shape)
    return ((j & 63) << 1) | (j >> 6)


def join_index(shape):
    j = lane_of(shape)
    return ((j & 1) << 6) | (j >> 1)


class Blocker:
    def __init__(self, half):
        s = row_of((8, 128))
        j = lane_of((8, 128))
        self.half = half
        self.stay = (s < 4) == ((j & (2 * half - 1)) < half)
        self.to = ((s & 1) << 2) | (s >> 1)
        self.back = ((s & 3) << 1) | (s >> 2)

    def swap(self, v):
        return jnp.where(self.stay, v, pltpu.roll(pltpu.roll(v, 4, 0), self.half, 1))

    def forward(self, v):
        return take_rows(self.swap(v), self.to)

    def inverse(self, v):
        return self.swap(take_rows(v, self.back))


def dot(a, b):
    return lax.dot_general(a, b, (((1,), (0,)), ((), ())), preferred_element_type=F32)


def block_product(x, high, low, layer):
    x_high = x.astype(BF16)
    x_low = (x - x_high.astype(F32)).astype(BF16)
    total = jnp.zeros(x.shape, F32)
    for index in range(high.shape[0]):
        part = dot(high[index], x_high) + dot(low[index], x_high) + dot(high[index], x_low)
        total = jnp.where(layer == index, part, total)
    return total


def fine_layers(depth_ref):
    v = depth_ref[...]
    return jnp.concatenate([v, v, v, v], axis=1)


def coarse_layers(depth_ref):
    v = depth_ref[...]
    v = jnp.broadcast_to(jnp.concatenate([v, v], axis=1), (8, 128))
    return take_lanes(v, (lane_of((8, 128)) & 31) << 1)[0:1]


def fine_columns(blocker, get, put):
    for c in range(6):
        for x in range(8):
            v = get(c, x)
            for t in range(2):
                put(c * 32 + (x % 4) * 8, ((x // 4) * 2 + t) * 128, blocker.forward(v[8 * t : 8 * t + 8]))


def fine_smooth(blocker, columns, high, low, layer, put):
    for bx in range(2):
        total = block_product(columns[:, bx * 256 : bx * 256 + 256], high, low, layer) * damping
        for c in range(6):
            for x in range(4):
                row = c * 32 + x * 8
                for t in range(2):
                    put(c, 4 * bx + x, t, blocker.inverse(total[row : row + 8, 128 * t : 128 * t + 128]))


def store_columns(columns):
    def put(row, lane, v):
        columns[row : row + 8, lane : lane + 128] = v

    return put


def coarse_smooth(blocker, columns, get, high, low, layer):
    for c in range(6):
        for x in range(4):
            row = c * 32 + x * 8
            columns[row : row + 8, :] = blocker.forward(get(c, x))
    total = block_product(columns[...], high, low, layer) * (damping * 4.0)
    return lambda c, x: blocker.inverse(total[c * 32 + x * 8 : c * 32 + x * 8 + 8])


def first_kernel(source, depth, inverses, x0, high, low, x_near, x_far, y_near, y_far, columns):
    blocker = Blocker(64)
    for index in range(8):
        m = inverses[index]
        m_high = m.astype(BF16)
        high[index] = m_high
        low[index] = (m - m_high.astype(F32)).astype(BF16)
    split = split_index((16, 128))
    fine_columns(blocker, lambda c, x: take_lanes(source[c, x], split), store_columns(columns))

    def put(c, x, t, v):
        x0[c, x, 8 * t : 8 * t + 8, :] = v

    fine_smooth(blocker, columns, high, low, fine_layers(depth), put)
    for c in range(6):
        x_near[c], x_far[c] = near_far("gx", x0[c, 0], x0[c, 7])
        y_near[c], y_far[c] = near_far("gy", x0[c, :, 0, :], x0[c, :, 15, :])


def around(u, y_before, y_after, half, other, keep, row):
    size = u.shape[0]
    before = jnp.where(row == 0, y_before, pltpu.roll(u, 1, 0))
    after = jnp.where(row == size - 1, y_after, pltpu.roll(u, size - 1, 0))
    return before + after + pltpu.roll(u, half, 1) + jnp.where(keep, take_lanes(u, other), 0.0)


def fine_other(shape):
    j = lane_of(shape)
    return jnp.where(j < 64, jnp.maximum(j + 63, 64), jnp.minimum(j - 63, 63)), (j != 0) & (j != 127)


def coarse_other(shape):
    j = lane_of(shape) & 63
    return jnp.where(j < 32, jnp.maximum(j + 31, 32), jnp.minimum(j - 31, 31)), (j != 0) & (j != 63)


def second_kernel(
    conductivity, source, classes, depth, x0, x_near_in, x_far_in, y_near_in, y_far_in, high, low,
    r0, b1, x1, sigma0, sigma1, x_near, x_far, y_near, y_far, rows, columns,
):
    x_halo = [before_after("gx", x_near_in[c], x_far_in[c]) for c in range(6)]
    y_halo = [before_after("gy", y_near_in[c], y_far_in[c]) for c in range(6)]
    shape = (16, 128)
    split = split_index(shape)
    other, keep = fine_other(shape)
    row = row_of(shape)
    j = lane_of(shape)
    pair = ((j & 31) << 1) | ((j >> 5) & 1)

    def restrict(v, slot):
        rows[slot] = take_lanes(v + pltpu.roll(v, 64, 1), pair)
        return (rows[slot, pl.ds(0, 8, stride=2), :] + rows[slot, pl.ds(1, 8, stride=2), :]) * 0.125

    for xx in range(4):
        sums = [None] * 7
        for x in (2 * xx, 2 * xx + 1):
            kind = take_lanes(classes[x], split)
            sigma = jnp.zeros(shape, F32)
            for index in range(8):
                sigma = jnp.where(kind == index, conductivity[index], sigma)
            sigma0[x] = sigma
            for c in range(3):
                re = x0[c, x]
                im = x0[c + 3, x]
                for comp, u, turn in ((c, re, -im), (c + 3, im, re)):
                    beside = around(
                        u, y_halo[comp][0][x : x + 1], y_halo[comp][1][x : x + 1], 64, other, keep, row
                    )
                    beside = beside + (x0[comp, x - 1] if x > 0 else x_halo[comp][0])
                    beside = beside + (x0[comp, x + 1] if x < 7 else x_halo[comp][1])
                    rest = take_lanes(source[comp, x], split) - (6.0 * u - beside + sigma * turn)
                    r0[comp, x] = rest
                    sums[comp] = rest if sums[comp] is None else sums[comp] + rest
            sums[6] = sigma if sums[6] is None else sums[6] + sigma
        for c in range(6):
            b1[c, xx] = restrict(sums[c], xx * 7 + c)
        sigma1[xx] = restrict(sums[6], xx * 7 + 6)
    result = coarse_smooth(Blocker(32), columns, lambda c, x: b1[c, x], high, low, coarse_layers(depth))
    store_coarse(result, x1, x_near, x_far, y_near, y_far)


def store_coarse(result, x1, x_near, x_far, y_near, y_far):
    for c in range(6):
        for x in range(4):
            x1[c, x] = result(c, x)
        x_near[c], x_far[c] = near_far("gx", x1[c, 0], x1[c, 3])
        y_near[c], y_far[c] = near_far("gy", x1[c, :, 0, :], x1[c, :, 7, :])


def middle_kernel(depth, x0, r0, high, low, y0, columns):
    blocker = Blocker(64)
    fine_columns(blocker, lambda c, x: r0[c, x], store_columns(columns))

    def put(c, x, t, v):
        y0[c, x, 8 * t : 8 * t + 8, :] = x0[c, x, 8 * t : 8 * t + 8, :] + v

    fine_smooth(blocker, columns, high, low, fine_layers(depth), put)


def third_kernel(
    depth, b1, x1a, sigma1, x_near_in, x_far_in, y_near_in, y_far_in, high, low,
    x1, x_near, x_far, y_near, y_far, columns,
):
    x_halo = [before_after("gx", x_near_in[c], x_far_in[c]) for c in range(6)]
    y_halo = [before_after("gy", y_near_in[c], y_far_in[c]) for c in range(6)]
    shape = (8, 128)
    other, keep = coarse_other(shape)
    row = row_of(shape)

    def residual(c, x):
        u = x1a[c, x]
        turn = -x1a[c + 3, x] if c < 3 else x1a[c - 3, x]
        beside = around(u, y_halo[c][0][x : x + 1], y_halo[c][1][x : x + 1], 32, other, keep, row)
        beside = beside + (x1a[c, x - 1] if x > 0 else x_halo[c][0])
        beside = beside + (x1a[c, x + 1] if x < 3 else x_halo[c][1])
        return b1[c, x] - ((6.0 * u - beside) * 0.25 + sigma1[x] * turn)

    more = coarse_smooth(Blocker(32), columns, residual, high, low, coarse_layers(depth))
    store_coarse(lambda c, x: x1a[c, x] + more(c, x), x1, x_near, x_far, y_near, y_far)


def last_kernel(
    depth, y0, x1, sigma0, x_near_in, x_far_in, y_near_in, y_far_in, high, low, out, coarse, image, base, columns
):
    x_halo = [before_after("gx", x_near_in[c], x_far_in[c]) for c in range(6)]
    y_halo = [before_after("gy", y_near_in[c], y_far_in[c]) for c in range(6)]
    shape = (8, 128)
    j = lane_of(shape)
    row = row_of(shape)
    k = j & 63
    self_index = ((k & 1) << 5) | (k >> 1)
    beyond = jnp.where(j < 64, k - 1, k + 1)
    inside = (beyond >= 0) & (beyond < 64)
    beyond = jnp.clip(beyond, 0, 63)
    next_index = ((beyond & 1) << 5) | (beyond >> 1)

    for c in range(6):
        coarse[c, 0] = take_lanes(x_halo[c][0], self_index)
        coarse[c, 5] = take_lanes(x_halo[c][1], self_index)
        for x in range(4):
            coarse[c, x + 1] = take_lanes(x1[c, x], self_index)
    for xx in range(4):
        for c in range(3):
            own = {}
            for comp in (c, c + 3):
                v = coarse[comp, xx + 1]
                beside = jnp.where(inside, take_lanes(x1[comp, xx], next_index), 0.0)
                low_y = take_lanes(jnp.broadcast_to(y_halo[comp][0][xx : xx + 1], shape), self_index)
                high_y = take_lanes(jnp.broadcast_to(y_halo[comp][1][xx : xx + 1], shape), self_index)
                before = jnp.where(row == 0, low_y, pltpu.roll(v, 1, 0))
                after = jnp.where(row == 7, high_y, pltpu.roll(v, 7, 0))
                own[comp] = (v, 3.0 * v - beside, before, after)
            for half in range(2):
                x = 2 * xx + half
                for parity in range(2):
                    sigma = sigma0[x, pl.ds(parity, 8, stride=2), :]
                    for comp, partner, sign in ((c, c + 3, -1.0), (c + 3, c, 1.0)):
                        v, kept, before, after = own[comp]
                        turned = kept - coarse[comp, xx + 2 * half] - (before, after)[parity]
                        value = turned + sign * sigma * own[partner][0]
                        image[comp, x, pl.ds(parity, 8, stride=2), :] = value
            for comp in (c, c + 3):
                base[comp, xx, pl.ds(0, 8, stride=2), :] = own[comp][0]
                base[comp, xx, pl.ds(1, 8, stride=2), :] = own[comp][0]

    blocker = Blocker(64)
    fine_columns(blocker, lambda c, x: image[c, x], store_columns(columns))
    join = join_index(shape)

    def put(c, x, t, v):
        part = slice(8 * t, 8 * t + 8)
        out[c, x, part, :] = take_lanes(y0[c, x, part, :] + base[c, x // 2, part, :] - v, join)

    fine_smooth(blocker, columns, high, low, fine_layers(depth), put)


def call(kernel, outs, args, scratch, scalars=0, outside=1, last=False):
    vmem = pl.BlockSpec(memory_space=pltpu.VMEM)
    smem = pl.BlockSpec(memory_space=pltpu.SMEM)
    args = list(args[:outside]) + [pltpu.with_memory_space_constraint(arg, pltpu.VMEM) for arg in args[outside:]]
    return pl.pallas_call(
        kernel,
        out_shape=[jax.ShapeDtypeStruct(*out) if last else pltpu.VMEM(*out) for out in outs],
        in_specs=[smem] * scalars + [vmem] * (len(args) - scalars),
        out_specs=[vmem] * len(outs),
        scratch_shapes=[pltpu.VMEM(shape, F32) for shape in scratch],
        compiler_params=pltpu.CompilerParams(vmem_limit_bytes=12 << 20),
        name=kernel.__name__,
    )(*args)


def exchange(x_near, x_far, y_near, y_far):
    def swapped(array, axis, first):
        size = lax.axis_size(axis)
        pairs = [(i, (i + 1) % size) for i in range(first, size, 2)]
        return lax.ppermute(array, axis, pairs + [(j, i) for i, j in pairs])

    y_near = swapped(y_near, "gy", 0)
    x_near = swapped(x_near, "gx", 0)
    y_far = swapped(y_far, "gy", 1)
    x_far = swapped(x_far, "gx", 1)
    return x_near, x_far, y_near, y_far


def near_far(axis, first, last):
    even = lax.axis_index(axis) % 2 == 0
    return jnp.where(even, last, first), jnp.where(even, first, last)


def before_after(axis, near, far):
    place = lax.axis_index(axis)
    even = place % 2 == 0
    before = jnp.where(place > 0, jnp.where(even, far, near), 0.0)
    after = jnp.where(place < lax.axis_size(axis) - 1, jnp.where(even, near, far), 0.0)
    return before, after


def per_device(source, cell_class, class_conductivity, layer_of_depth, inverses):
    depth = layer_of_depth.reshape(1, 64)
    fine = ((6, 8, 16, 128), F32)
    coarse = ((6, 4, 8, 128), F32)
    matrices = ((8, 192, 192), BF16)
    fine_faces = [((6, 16, 128), F32)] * 2 + [((6, 8, 128), F32)] * 2
    coarse_faces = [((6, 8, 128), F32)] * 2 + [((6, 4, 128), F32)] * 2

    x0, high, low, *faces = call(
        first_kernel, [fine, matrices, matrices] + fine_faces, (source, depth, inverses), [(192, 512)], outside=3
    )
    halos = exchange(*faces)
    r0, b1, x1a, sigma0, sigma1, *faces = call(
        second_kernel,
        [fine, coarse, coarse, ((8, 16, 128), F32), ((4, 8, 128), F32)] + coarse_faces,
        (class_conductivity, source, cell_class, depth, x0, *halos, high, low),
        [(28, 16, 128), (192, 128)],
        scalars=1,
        outside=4,
    )
    halos = exchange(*faces)
    (y0,) = call(middle_kernel, [fine], (depth, x0, r0, high, low), [(192, 512)])
    x1, *faces = call(
        third_kernel, [coarse] + coarse_faces, (depth, b1, x1a, sigma1, *halos, high, low), [(192, 128)]
    )
    halos = exchange(*faces)
    (out,) = call(
        last_kernel,
        [fine],
        (depth, y0, x1, sigma0, *halos, high, low),
        [(6, 6, 8, 128), (6, 8, 16, 128), (6, 4, 16, 128), (192, 512)],
        last=True,
    )
    return out


def solution(mesh):
    placed = (P(None, "gx", "gy", None), P("gx", "gy", None), P(), P(), P())
    return jax.shard_map(
        per_device, mesh=mesh, in_specs=placed, out_specs=P(None, "gx", "gy", None), check_vma=False
    )
```

```python
import jax
import jax.numpy as jnp
from jax import lax
from jax.experimental import pallas as pl
from jax.experimental.pallas import tpu as pltpu
from jax.sharding import PartitionSpec as P

damping = 0.8
F32 = jnp.float32
BF16 = jnp.bfloat16


def lane_of(shape):
    return lax.broadcasted_iota(jnp.int32, shape, 1)


def row_of(shape):
    return lax.broadcasted_iota(jnp.int32, shape, 0)


def take_lanes(v, index):
    return jnp.take_along_axis(v, index, axis=1, mode="promise_in_bounds")


def take_rows(v, index):
    return jnp.take_along_axis(v, index, axis=0, mode="promise_in_bounds")


def split_index(shape):
    j = lane_of(shape)
    return ((j & 63) << 1) | (j >> 6)


def join_index(shape):
    j = lane_of(shape)
    return ((j & 1) << 6) | (j >> 1)


class Blocker:
    def __init__(self, half):
        s = row_of((8, 128))
        j = lane_of((8, 128))
        self.half = half
        self.stay = (s < 4) == ((j & (2 * half - 1)) < half)
        self.to = ((s & 1) << 2) | (s >> 1)
        self.back = ((s & 3) << 1) | (s >> 2)

    def swap(self, v):
        return jnp.where(self.stay, v, pltpu.roll(pltpu.roll(v, 4, 0), self.half, 1))

    def forward(self, v):
        return take_rows(self.swap(v), self.to)

    def inverse(self, v):
        return self.swap(take_rows(v, self.back))


def dot(a, b):
    return lax.dot_general(a, b, (((1,), (0,)), ((), ())), preferred_element_type=F32)


def block_product(x, high, low, layer):
    x_high = x.astype(BF16)
    x_low = (x - x_high.astype(F32)).astype(BF16)
    total = jnp.zeros(x.shape, F32)
    for index in range(high.shape[0]):
        part = dot(high[index], x_high) + dot(low[index], x_high) + dot(high[index], x_low)
        total = jnp.where(layer == index, part, total)
    return total


def fine_layers(depth_ref):
    v = depth_ref[...]
    return jnp.concatenate([v, v, v, v], axis=1)


def coarse_layers(depth_ref):
    v = depth_ref[...]
    v = jnp.broadcast_to(jnp.concatenate([v, v], axis=1), (8, 128))
    return take_lanes(v, (lane_of((8, 128)) & 31) << 1)[0:1]


def fine_columns(blocker, get, put):
    for c in range(6):
        for x in range(8):
            v = get(c, x)
            for t in range(2):
                put(c * 32 + (x % 4) * 8, ((x // 4) * 2 + t) * 128, blocker.forward(v[8 * t : 8 * t + 8]))


def fine_smooth(blocker, columns, high, low, layer, put):
    for bx in range(2):
        total = block_product(columns[:, bx * 256 : bx * 256 + 256], high, low, layer) * damping
        for c in range(6):
            for x in range(4):
                row = c * 32 + x * 8
                for t in range(2):
                    put(c, 4 * bx + x, t, blocker.inverse(total[row : row + 8, 128 * t : 128 * t + 128]))


def store_columns(columns):
    def put(row, lane, v):
        columns[row : row + 8, lane : lane + 128] = v

    return put


def coarse_smooth(blocker, columns, get, high, low, layer):
    for c in range(6):
        for x in range(4):
            row = c * 32 + x * 8
            columns[row : row + 8, :] = blocker.forward(get(c, x))
    total = block_product(columns[...], high, low, layer) * (damping * 4.0)
    return lambda c, x: blocker.inverse(total[c * 32 + x * 8 : c * 32 + x * 8 + 8])


def first_kernel(
    source_hbm, depth_hbm, inverses_hbm, x0, b0, high, low, layers, y_near, x_near, y_far, x_far,
    source, depth, inverses, columns, done,
):
    copies = [
        pltpu.make_async_copy(source_hbm, source, done.at[0]),
        pltpu.make_async_copy(depth_hbm, depth, done.at[1]),
    ]
    for index in range(8):
        copies.append(pltpu.make_async_copy(inverses_hbm.at[index], inverses.at[index], done.at[2 + index]))
    for copy in copies:
        copy.start()
    blocker = Blocker(64)
    split = split_index((16, 128))
    copies[0].wait()

    def get(c, x):
        v = take_lanes(source[c, x], split)
        b0[c, x] = v
        return v

    fine_columns(blocker, get, store_columns(columns))
    copies[1].wait()
    layers[0:1, :] = fine_layers(depth)
    layers[1:2, 0:128] = coarse_layers(depth)
    for index in range(8):
        copies[2 + index].wait()
        m = inverses[index]
        m_high = m.astype(BF16)
        high[index] = m_high
        low[index] = (m - m_high.astype(F32)).astype(BF16)

    def put(c, x, t, v):
        x0[c, x, 8 * t : 8 * t + 8, :] = v

    fine_smooth(blocker, columns, high, low, layers[0:1, :], put)
    for c in range(6):
        x_near[c], x_far[c] = near_far("gx", x0[c, 0], x0[c, 7])
        y_near[c, 0:8], y_far[c, 0:8] = near_far("gy", x0[c, :, 0, :], x0[c, :, 15, :])
        y_near[c, 8:16] = y_near[c, 0:8]
        y_far[c, 8:16] = y_far[c, 0:8]


def around(u, y_before, y_after, half, other, keep, row):
    size = u.shape[0]
    before = jnp.where(row == 0, y_before, pltpu.roll(u, 1, 0))
    after = jnp.where(row == size - 1, y_after, pltpu.roll(u, size - 1, 0))
    return before + after + pltpu.roll(u, half, 1) + jnp.where(keep, take_lanes(u, other), 0.0)


def fine_other(shape):
    j = lane_of(shape)
    return jnp.where(j < 64, jnp.maximum(j + 63, 64), jnp.minimum(j - 63, 63)), (j != 0) & (j != 127)


def coarse_other(shape):
    j = lane_of(shape) & 63
    return jnp.where(j < 32, jnp.maximum(j + 31, 32), jnp.minimum(j - 31, 31)), (j != 0) & (j != 63)


def second_kernel(
    conductivity, classes, b0, layers, x0, y_near_in, x_near_in, y_far_in, x_far_in, high, low,
    r0, b1, x1, sigma0, sigma1, y_near, x_near, y_far, x_far, rows, columns,
):
    x_halo = [before_after("gx", x_near_in[c], x_far_in[c]) for c in range(6)]
    y_halo = [before_after("gy", y_near_in[c], y_far_in[c]) for c in range(6)]
    shape = (16, 128)
    split = split_index(shape)
    other, keep = fine_other(shape)
    row = row_of(shape)
    j = lane_of(shape)
    pair = ((j & 31) << 1) | ((j >> 5) & 1)

    def restrict(v, slot):
        rows[slot] = take_lanes(v + pltpu.roll(v, 64, 1), pair)
        return (rows[slot, pl.ds(0, 8, stride=2), :] + rows[slot, pl.ds(1, 8, stride=2), :]) * 0.125

    for xx in range(4):
        sums = [None] * 7
        for x in (2 * xx, 2 * xx + 1):
            kind = take_lanes(classes[x], split)
            sigma = jnp.zeros(shape, F32)
            for index in range(8):
                sigma = jnp.where(kind == index, conductivity[index], sigma)
            sigma0[x] = sigma
            for c in range(3):
                re = x0[c, x]
                im = x0[c + 3, x]
                for comp, u, turn in ((c, re, -im), (c + 3, im, re)):
                    beside = around(
                        u, y_halo[comp][0][x : x + 1], y_halo[comp][1][x : x + 1], 64, other, keep, row
                    )
                    beside = beside + (x0[comp, x - 1] if x > 0 else x_halo[comp][0])
                    beside = beside + (x0[comp, x + 1] if x < 7 else x_halo[comp][1])
                    rest = b0[comp, x] - (6.0 * u - beside + sigma * turn)
                    r0[comp, x] = rest
                    sums[comp] = rest if sums[comp] is None else sums[comp] + rest
            sums[6] = sigma if sums[6] is None else sums[6] + sigma
        for c in range(6):
            b1[c, xx] = restrict(sums[c], xx * 7 + c)
        sigma1[xx] = restrict(sums[6], xx * 7 + 6)
    result = coarse_smooth(Blocker(32), columns, lambda c, x: b1[c, x], high, low, layers[1:2, 0:128])
    store_coarse(result, x1, y_near, x_near, y_far, x_far)


def store_coarse(result, x1, y_near, x_near, y_far, x_far):
    for c in range(6):
        for x in range(4):
            x1[c, x] = result(c, x)
        x_near[c], x_far[c] = near_far("gx", x1[c, 0], x1[c, 3])
        y_near[c, 0:4], y_far[c, 0:4] = near_far("gy", x1[c, :, 0, :], x1[c, :, 7, :])
        y_near[c, 4:8] = y_near[c, 0:4]
        y_far[c, 4:8] = y_far[c, 0:4]


def middle_kernel(layers, x0, r0, high, low, y0, columns):
    blocker = Blocker(64)
    fine_columns(blocker, lambda c, x: r0[c, x], store_columns(columns))

    def put(c, x, t, v):
        y0[c, x, 8 * t : 8 * t + 8, :] = x0[c, x, 8 * t : 8 * t + 8, :] + v

    fine_smooth(blocker, columns, high, low, layers[0:1, :], put)


def third_kernel(
    layers, b1, x1a, sigma1, y_near_in, x_near_in, y_far_in, x_far_in, high, low,
    x1, y_near, x_near, y_far, x_far, columns,
):
    x_halo = [before_after("gx", x_near_in[c], x_far_in[c]) for c in range(6)]
    y_halo = [before_after("gy", y_near_in[c], y_far_in[c]) for c in range(6)]
    shape = (8, 128)
    other, keep = coarse_other(shape)
    row = row_of(shape)

    def residual(c, x):
        u = x1a[c, x]
        turn = -x1a[c + 3, x] if c < 3 else x1a[c - 3, x]
        beside = around(u, y_halo[c][0][x : x + 1], y_halo[c][1][x : x + 1], 32, other, keep, row)
        beside = beside + (x1a[c, x - 1] if x > 0 else x_halo[c][0])
        beside = beside + (x1a[c, x + 1] if x < 3 else x_halo[c][1])
        return b1[c, x] - ((6.0 * u - beside) * 0.25 + sigma1[x] * turn)

    more = coarse_smooth(Blocker(32), columns, residual, high, low, layers[1:2, 0:128])
    store_coarse(lambda c, x: x1a[c, x] + more(c, x), x1, y_near, x_near, y_far, x_far)


def last_kernel(
    layers, y0, x1, sigma0, y_near_in, x_near_in, y_far_in, x_far_in, high, low, out, coarse, image, base, columns
):
    x_halo = [before_after("gx", x_near_in[c], x_far_in[c]) for c in range(6)]
    y_halo = [before_after("gy", y_near_in[c], y_far_in[c]) for c in range(6)]
    shape = (8, 128)
    j = lane_of(shape)
    row = row_of(shape)
    k = j & 63
    self_index = ((k & 1) << 5) | (k >> 1)
    beyond = jnp.where(j < 64, k - 1, k + 1)
    inside = (beyond >= 0) & (beyond < 64)
    beyond = jnp.clip(beyond, 0, 63)
    next_index = ((beyond & 1) << 5) | (beyond >> 1)

    for c in range(6):
        coarse[c, 0] = take_lanes(x_halo[c][0], self_index)
        coarse[c, 5] = take_lanes(x_halo[c][1], self_index)
        for x in range(4):
            coarse[c, x + 1] = take_lanes(x1[c, x], self_index)
    for xx in range(4):
        for c in range(3):
            own = {}
            for comp in (c, c + 3):
                v = coarse[comp, xx + 1]
                beside = jnp.where(inside, take_lanes(x1[comp, xx], next_index), 0.0)
                low_y = take_lanes(jnp.broadcast_to(y_halo[comp][0][xx : xx + 1], shape), self_index)
                high_y = take_lanes(jnp.broadcast_to(y_halo[comp][1][xx : xx + 1], shape), self_index)
                before = jnp.where(row == 0, low_y, pltpu.roll(v, 1, 0))
                after = jnp.where(row == 7, high_y, pltpu.roll(v, 7, 0))
                own[comp] = (v, 3.0 * v - beside, before, after)
            for half in range(2):
                x = 2 * xx + half
                for parity in range(2):
                    sigma = sigma0[x, pl.ds(parity, 8, stride=2), :]
                    for comp, partner, sign in ((c, c + 3, -1.0), (c + 3, c, 1.0)):
                        v, kept, before, after = own[comp]
                        turned = kept - coarse[comp, xx + 2 * half] - (before, after)[parity]
                        value = turned + sign * sigma * own[partner][0]
                        image[comp, x, pl.ds(parity, 8, stride=2), :] = value
            for comp in (c, c + 3):
                base[comp, xx, pl.ds(0, 8, stride=2), :] = own[comp][0]
                base[comp, xx, pl.ds(1, 8, stride=2), :] = own[comp][0]

    blocker = Blocker(64)
    fine_columns(blocker, lambda c, x: image[c, x], store_columns(columns))
    join = join_index(shape)

    def put(c, x, t, v):
        part = slice(8 * t, 8 * t + 8)
        out[c, x, part, :] = take_lanes(y0[c, x, part, :] + base[c, x // 2, part, :] - v, join)

    fine_smooth(blocker, columns, high, low, layers[0:1, :], put)


def call(kernel, outs, args, scratch, spaces=(), last=False):
    vmem = pl.BlockSpec(memory_space=pltpu.VMEM)
    own = len(spaces)
    args = [pltpu.with_memory_space_constraint(arg, space) for arg, space in zip(args, spaces)] + [pltpu.with_memory_space_constraint(arg, pltpu.VMEM) for arg in args[own:]]
    return pl.pallas_call(
        kernel,
        out_shape=[jax.ShapeDtypeStruct(*out) if last else pltpu.VMEM(*out) for out in outs],
        in_specs=[pl.BlockSpec(memory_space=space) for space in spaces] + [vmem] * (len(args) - own),
        out_specs=[vmem] * len(outs),
        scratch_shapes=scratch,
        compiler_params=pltpu.CompilerParams(vmem_limit_bytes=12 << 20),
        name=kernel.__name__,
    )(*args)


def exchange(y_near, x_near, y_far, x_far):
    def swapped(array, axis, first):
        size = lax.axis_size(axis)
        pairs = [(i, i + 1) for i in range(first, size - 1, 2)]
        alone = [(i, i) for i in (0, size - 1) if first == 1]
        return lax.ppermute(array, axis, pairs + [(j, i) for i, j in pairs] + alone)

    y_near = swapped(y_near, "gy", 0)
    x_near = swapped(x_near, "gx", 0)
    y_far = swapped(y_far, "gy", 1)
    x_far = swapped(x_far, "gx", 1)
    return y_near, x_near, y_far, x_far


def near_far(axis, first, last):
    even = lax.axis_index(axis) % 2 == 0
    return jnp.where(even, last, first), jnp.where(even, first, last)


def before_after(axis, near, far):
    place = lax.axis_index(axis)
    even = place % 2 == 0
    before = jnp.where(place > 0, jnp.where(even, far, near), 0.0)
    after = jnp.where(place < lax.axis_size(axis) - 1, jnp.where(even, near, far), 0.0)
    return before, after


def per_device(source, cell_class, class_conductivity, layer_of_depth, inverses):
    fine = ((6, 8, 16, 128), F32)
    coarse = ((6, 4, 8, 128), F32)
    matrices = ((8, 192, 192), BF16)
    fine_faces = [((6, 16, 128), F32)] * 4
    coarse_faces = [((6, 8, 128), F32)] * 4
    columns = pltpu.VMEM((192, 512), F32)
    coarse_columns = pltpu.VMEM((192, 128), F32)

    x0, b0, high, low, layers, *faces = call(
        first_kernel,
        [fine, fine, matrices, matrices, ((8, 256), jnp.int32)] + fine_faces,
        (source, layer_of_depth.reshape(1, 64), inverses),
        [
            pltpu.VMEM(source.shape, F32),
            pltpu.VMEM((1, 64), jnp.int32),
            pltpu.VMEM(inverses.shape, F32),
            columns,
            pltpu.SemaphoreType.DMA((10,)),
        ],
        spaces=(pltpu.HBM,) * 3,
    )
    halos = exchange(*faces)
    r0, b1, x1a, sigma0, sigma1, *faces = call(
        second_kernel,
        [fine, coarse, coarse, ((8, 16, 128), F32), ((4, 8, 128), F32)] + coarse_faces,
        (class_conductivity, cell_class, b0, layers, x0, *halos, high, low),
        [pltpu.VMEM((28, 16, 128), F32), coarse_columns],
        spaces=(pltpu.SMEM, pltpu.VMEM),
    )
    halos = exchange(*faces)
    (y0,) = call(middle_kernel, [fine], (layers, x0, r0, high, low), [columns])
    x1, *faces = call(
        third_kernel, [coarse] + coarse_faces, (layers, b1, x1a, sigma1, *halos, high, low), [coarse_columns]
    )
    halos = exchange(*faces)
    (out,) = call(
        last_kernel,
        [fine],
        (layers, y0, x1, sigma0, *halos, high, low),
        [pltpu.VMEM((6, 6, 8, 128), F32), pltpu.VMEM(*fine), pltpu.VMEM((6, 4, 16, 128), F32), columns],
        last=True,
    )
    return out


def solution(mesh):
    placed = (P(None, "gx", "gy", None), P("gx", "gy", None), P(), P(), P())
    return jax.shard_map(
        per_device, mesh=mesh, in_specs=placed, out_specs=P(None, "gx", "gy", None), check_vma=False
    )
```

```python
import jax
import jax.numpy as jnp
from jax import lax
from jax.experimental import pallas as pl
from jax.experimental.pallas import tpu as pltpu
from jax.sharding import PartitionSpec as P

damping = 0.8
F32 = jnp.float32
BF16 = jnp.bfloat16


def lane_of(shape):
    return lax.broadcasted_iota(jnp.int32, shape, 1)


def row_of(shape):
    return lax.broadcasted_iota(jnp.int32, shape, 0)


def take_lanes(v, index):
    return jnp.take_along_axis(v, index, axis=1, mode="promise_in_bounds")


def take_rows(v, index):
    return jnp.take_along_axis(v, index, axis=0, mode="promise_in_bounds")


def split_index(shape):
    j = lane_of(shape)
    return ((j & 63) << 1) | (j >> 6)


def join_index(shape):
    j = lane_of(shape)
    return ((j & 1) << 6) | (j >> 1)


class Blocker:
    def __init__(self, half):
        s = row_of((8, 128))
        j = lane_of((8, 128))
        self.half = half
        self.stay = (s < 4) == ((j & (2 * half - 1)) < half)
        self.to = ((s & 1) << 2) | (s >> 1)
        self.back = ((s & 3) << 1) | (s >> 2)

    def swap(self, v):
        return jnp.where(self.stay, v, pltpu.roll(pltpu.roll(v, 4, 0), self.half, 1))

    def forward(self, v):
        return take_rows(self.swap(v), self.to)

    def inverse(self, v):
        return self.swap(take_rows(v, self.back))


def dot(a, b):
    return lax.dot_general(a, b, (((1,), (0,)), ((), ())), preferred_element_type=F32)


def block_product(x, high, low, layer):
    x_high = x.astype(BF16)
    x_low = (x - x_high.astype(F32)).astype(BF16)
    total = jnp.zeros(x.shape, F32)
    for index in range(high.shape[0]):
        part = dot(high[index], x_high) + dot(low[index], x_high) + dot(high[index], x_low)
        total = jnp.where(layer == index, part, total)
    return total


def fine_layers(depth_ref):
    v = depth_ref[...]
    return jnp.concatenate([v, v, v, v], axis=1)


def coarse_layers(depth_ref):
    v = depth_ref[...]
    v = jnp.broadcast_to(jnp.concatenate([v, v], axis=1), (8, 128))
    return take_lanes(v, (lane_of((8, 128)) & 31) << 1)[0:1]


def fine_columns(blocker, get, put):
    for c in range(6):
        for x in range(8):
            v = get(c, x)
            for t in range(2):
                put(c * 32 + (x % 4) * 8, ((x // 4) * 2 + t) * 128, blocker.forward(v[8 * t : 8 * t + 8]))


def fine_smooth(blocker, columns, high, low, layer, put):
    for bx in range(2):
        total = block_product(columns[:, bx * 256 : bx * 256 + 256], high, low, layer) * damping
        for c in range(6):
            for x in range(4):
                row = c * 32 + x * 8
                for t in range(2):
                    put(c, 4 * bx + x, t, blocker.inverse(total[row : row + 8, 128 * t : 128 * t + 128]))


def store_columns(columns):
    def put(row, lane, v):
        columns[row : row + 8, lane : lane + 128] = v

    return put


def coarse_smooth(blocker, columns, get, high, low, layer):
    for c in range(6):
        for x in range(4):
            row = c * 32 + x * 8
            columns[row : row + 8, :] = blocker.forward(get(c, x))
    total = block_product(columns[...], high, low, layer) * (damping * 4.0)
    return lambda c, x: blocker.inverse(total[c * 32 + x * 8 : c * 32 + x * 8 + 8])


def first_kernel(
    source_hbm, depth_hbm, inverses_hbm, x0, b0, high, low, layers, x_near, x_far, y_near, y_far,
    source, depth, inverses, columns, done,
):
    copies = [
        pltpu.make_async_copy(source_hbm, source, done.at[0]),
        pltpu.make_async_copy(depth_hbm, depth, done.at[1]),
        pltpu.make_async_copy(inverses_hbm, inverses, done.at[2]),
    ]
    for copy in copies:
        copy.start()
    blocker = Blocker(64)
    split = split_index((16, 128))
    copies[0].wait()

    def get(c, x):
        v = take_lanes(source[c, x], split)
        b0[c, x] = v
        return v

    fine_columns(blocker, get, store_columns(columns))
    copies[1].wait()
    layers[0:1, :] = fine_layers(depth)
    layers[1:2, 0:128] = coarse_layers(depth)
    copies[2].wait()
    for index in range(8):
        m = inverses[index]
        m_high = m.astype(BF16)
        high[index] = m_high
        low[index] = (m - m_high.astype(F32)).astype(BF16)

    def put(c, x, t, v):
        x0[c, x, 8 * t : 8 * t + 8, :] = v

    fine_smooth(blocker, columns, high, low, layers[0:1, :], put)
    for c in range(6):
        x_near[c], x_far[c] = near_far("gx", x0[c, 0], x0[c, 7])
        y_near[c, 0:8], y_far[c, 0:8] = near_far("gy", x0[c, :, 0, :], x0[c, :, 15, :])
        y_near[c, 8:16] = y_near[c, 0:8]
        y_far[c, 8:16] = y_far[c, 0:8]


def around(u, y_before, y_after, half, other, keep, row):
    size = u.shape[0]
    before = jnp.where(row == 0, y_before, pltpu.roll(u, 1, 0))
    after = jnp.where(row == size - 1, y_after, pltpu.roll(u, size - 1, 0))
    return before + after + pltpu.roll(u, half, 1) + jnp.where(keep, take_lanes(u, other), 0.0)


def fine_other(shape):
    j = lane_of(shape)
    return jnp.where(j < 64, jnp.maximum(j + 63, 64), jnp.minimum(j - 63, 63)), (j != 0) & (j != 127)


def coarse_other(shape):
    j = lane_of(shape) & 63
    return jnp.where(j < 32, jnp.maximum(j + 31, 32), jnp.minimum(j - 31, 31)), (j != 0) & (j != 63)


def pair_index(shape):
    j = lane_of(shape)
    return ((j & 31) << 1) | ((j >> 5) & 1)


def own_kernel(conductivity, classes, b0, x0, r0, b1, sigma0, sigma1, rows):
    shape = (16, 128)
    split = split_index(shape)
    other, keep = fine_other(shape)
    row = row_of(shape)
    pair = pair_index(shape)

    def restrict(v, slot):
        rows[slot] = take_lanes(v + pltpu.roll(v, 64, 1), pair)
        return (rows[slot, pl.ds(0, 8, stride=2), :] + rows[slot, pl.ds(1, 8, stride=2), :]) * 0.125

    for xx in range(4):
        sums = [None] * 7
        for x in (2 * xx, 2 * xx + 1):
            kind = take_lanes(classes[x], split)
            sigma = jnp.zeros(shape, F32)
            for index in range(8):
                sigma = jnp.where(kind == index, conductivity[index], sigma)
            sigma0[x] = sigma
            for c in range(3):
                re = x0[c, x]
                im = x0[c + 3, x]
                for comp, u, turn in ((c, re, -im), (c + 3, im, re)):
                    beside = around(u, 0.0, 0.0, 64, other, keep, row)
                    if x > 0:
                        beside = beside + x0[comp, x - 1]
                    if x < 7:
                        beside = beside + x0[comp, x + 1]
                    rest = b0[comp, x] - (6.0 * u - beside + sigma * turn)
                    r0[comp, x] = rest
                    sums[comp] = rest if sums[comp] is None else sums[comp] + rest
            sums[6] = sigma if sums[6] is None else sums[6] + sigma
        for c in range(6):
            b1[c, xx] = restrict(sums[c], xx * 7 + c)
        sigma1[xx] = restrict(sums[6], xx * 7 + 6)


def second_kernel(
    own_b1, layers, x_near_in, x_far_in, y_near_in, y_far_in, high, low,
    b1, x1, x_near, x_far, y_near, y_far, rows, columns,
):
    shape = (16, 128)
    pair = pair_index(shape)
    narrow = (8, 128)
    row = row_of(narrow)
    for c in range(6):
        added = []
        for side, v in enumerate(before_after("gx", x_near_in[c], x_far_in[c])):
            slot = 2 * c + side
            rows[slot] = take_lanes(v + pltpu.roll(v, 64, 1), pair)
            added.append((rows[slot, pl.ds(0, 8, stride=2), :] + rows[slot, pl.ds(1, 8, stride=2), :]) * 0.125)
        edges = []
        for v in before_after("gy", y_near_in[c, 0:8], y_far_in[c, 0:8]):
            v = take_lanes(v + pltpu.roll(v, 64, 1), pair[0:8])
            edges.append((v + pltpu.roll(v, 7, 0)) * 0.125)
        for x in range(4):
            v = own_b1[c, x] + jnp.where(row == 0, edges[0][2 * x : 2 * x + 1], 0.0)
            v = v + jnp.where(row == 7, edges[1][2 * x : 2 * x + 1], 0.0)
            if x == 0:
                v = v + added[0]
            if x == 3:
                v = v + added[1]
            b1[c, x] = v
    result = coarse_smooth(Blocker(32), columns, lambda c, x: b1[c, x], high, low, layers[1:2, 0:128])
    store_coarse(result, x1, x_near, x_far, y_near, y_far)


def store_coarse(result, x1, x_near, x_far, y_near, y_far):
    for c in range(6):
        for x in range(4):
            x1[c, x] = result(c, x)
        x_near[c], x_far[c] = near_far("gx", x1[c, 0], x1[c, 3])
        y_near[c, 0:4], y_far[c, 0:4] = near_far("gy", x1[c, :, 0, :], x1[c, :, 7, :])
        y_near[c, 4:8] = y_near[c, 0:4]
        y_far[c, 4:8] = y_far[c, 0:4]


def middle_kernel(layers, x0, r0, x_near_in, x_far_in, y_near_in, y_far_in, high, low, y0, columns):
    blocker = Blocker(64)
    row = row_of((16, 128))
    x_halo = [before_after("gx", x_near_in[c], x_far_in[c]) for c in range(6)]
    y_halo = [before_after("gy", y_near_in[c, 0:8], y_far_in[c, 0:8]) for c in range(6)]

    def get(c, x):
        v = r0[c, x] + jnp.where(row == 0, y_halo[c][0][x : x + 1], 0.0)
        v = v + jnp.where(row == 15, y_halo[c][1][x : x + 1], 0.0)
        if x == 0:
            v = v + x_halo[c][0]
        if x == 7:
            v = v + x_halo[c][1]
        return v

    fine_columns(blocker, get, store_columns(columns))

    def put(c, x, t, v):
        y0[c, x, 8 * t : 8 * t + 8, :] = x0[c, x, 8 * t : 8 * t + 8, :] + v

    fine_smooth(blocker, columns, high, low, layers[0:1, :], put)


def third_kernel(
    layers, y0, b1, x1a, sigma1, x_near_in, x_far_in, y_near_in, y_far_in, high, low,
    x1, x_near, x_far, y_near, y_far, columns,
):
    x_halo = [before_after("gx", x_near_in[c], x_far_in[c]) for c in range(6)]
    y_halo = [before_after("gy", y_near_in[c], y_far_in[c]) for c in range(6)]
    shape = (8, 128)
    other, keep = coarse_other(shape)
    row = row_of(shape)

    def residual(c, x):
        u = x1a[c, x]
        turn = -x1a[c + 3, x] if c < 3 else x1a[c - 3, x]
        beside = around(u, y_halo[c][0][x : x + 1], y_halo[c][1][x : x + 1], 32, other, keep, row)
        beside = beside + (x1a[c, x - 1] if x > 0 else x_halo[c][0])
        beside = beside + (x1a[c, x + 1] if x < 3 else x_halo[c][1])
        return b1[c, x] - ((6.0 * u - beside) * 0.25 + sigma1[x] * turn)

    more = coarse_smooth(Blocker(32), columns, residual, high, low, layers[1:2, 0:128])
    store_coarse(lambda c, x: x1a[c, x] + more(c, x), x1, x_near, x_far, y_near, y_far)


def self_index(shape):
    k = lane_of(shape) & 63
    return ((k & 1) << 5) | (k >> 1)


def prolong_kernel(x1, sigma0, y0, image, base, coarse, rows):
    shape = (8, 128)
    j = lane_of(shape)
    row = row_of(shape)
    k = j & 63
    beyond = jnp.where(j < 64, k - 1, k + 1)
    inside = (beyond >= 0) & (beyond < 64)
    beyond = jnp.clip(beyond, 0, 63)
    next_index = ((beyond & 1) << 5) | (beyond >> 1)
    own_index = self_index(shape)

    for c in range(6):
        for x in range(4):
            coarse[c, x] = take_lanes(x1[c, x], own_index)
    for xx in range(4):
        for c in range(3):
            own = {}
            for comp in (c, c + 3):
                v = coarse[comp, xx]
                beside = jnp.where(inside, take_lanes(x1[comp, xx], next_index), 0.0)
                before = jnp.where(row == 0, 0.0, pltpu.roll(v, 1, 0))
                after = jnp.where(row == 7, 0.0, pltpu.roll(v, 7, 0))
                own[comp] = (v, 3.0 * v - beside, before, after)
                rows[comp, xx, pl.ds(0, 8, stride=2), :] = v
                rows[comp, xx, pl.ds(1, 8, stride=2), :] = v
            for half in range(2):
                x = 2 * xx + half
                next_x = xx - 1 + 2 * half
                for parity in range(2):
                    sigma = sigma0[x, pl.ds(parity, 8, stride=2), :]
                    for comp, partner, sign in ((c, c + 3, -1.0), (c + 3, c, 1.0)):
                        v, kept, before, after = own[comp]
                        value = kept - (before, after)[parity] + sign * sigma * own[partner][0]
                        if 0 <= next_x < 4:
                            value = value - coarse[comp, next_x]
                        image[comp, x, pl.ds(parity, 8, stride=2), :] = value
                for comp in (c, c + 3):
                    base[comp, x] = y0[comp, x] + rows[comp, xx]


def last_kernel(layers, image, base, x_near_in, x_far_in, y_near_in, y_far_in, high, low, out, rows, columns):
    shape = (8, 128)
    own_index = self_index(shape)
    row = row_of((16, 128))
    y_halo = []
    for c in range(6):
        for side, v in enumerate(before_after("gx", x_near_in[c], x_far_in[c])):
            v = take_lanes(v, own_index)
            slot = 2 * c + side
            rows[slot, pl.ds(0, 8, stride=2), :] = v
            rows[slot, pl.ds(1, 8, stride=2), :] = v
        y_halo.append([take_lanes(v, own_index) for v in before_after("gy", y_near_in[c], y_far_in[c])])

    def get(c, x):
        v = image[c, x] - jnp.where(row == 0, y_halo[c][0][x // 2 : x // 2 + 1], 0.0)
        v = v - jnp.where(row == 15, y_halo[c][1][x // 2 : x // 2 + 1], 0.0)
        if x == 0:
            v = v - rows[2 * c]
        if x == 7:
            v = v - rows[2 * c + 1]
        return v

    blocker = Blocker(64)
    fine_columns(blocker, get, store_columns(columns))
    join = join_index(shape)

    def put(c, x, t, v):
        out[c, x, 8 * t : 8 * t + 8, :] = take_lanes(base[c, x, 8 * t : 8 * t + 8, :] - v, join)

    fine_smooth(blocker, columns, high, low, layers[0:1, :], put)


def call(kernel, outs, args, scratch, spaces=(), last=False):
    vmem = pl.BlockSpec(memory_space=pltpu.VMEM)
    own = len(spaces)
    args = [arg if space == pltpu.SMEM else pltpu.with_memory_space_constraint(arg, space) for arg, space in zip(args, spaces)] + [pltpu.with_memory_space_constraint(arg, pltpu.VMEM) for arg in args[own:]]
    return pl.pallas_call(
        kernel,
        out_shape=[jax.ShapeDtypeStruct(*out) if last else pltpu.VMEM(*out) for out in outs],
        in_specs=[pl.BlockSpec(memory_space=space) for space in spaces] + [vmem] * (len(args) - own),
        out_specs=[vmem] * len(outs),
        scratch_shapes=scratch,
        compiler_params=pltpu.CompilerParams(vmem_limit_bytes=12 << 20),
        name=kernel.__name__,
    )(*args)


def exchange(x_near, x_far, y_near, y_far):
    nx, ny = lax.axis_size("gx"), lax.axis_size("gy")

    def swapped(array, partner):
        pairs = [(i * ny + j, partner(i, j)) for i in range(nx) for j in range(ny)]
        return lax.ppermute(array, ("gx", "gy"), [(a, i * ny + j) for a, (i, j) in pairs])

    def far(i):
        return i + 1 if i % 2 else i - 1

    def x_far_partner(i, j):
        return (i, j ^ 1) if i in (0, nx - 1) else (far(i), j)

    def y_far_partner(i, j):
        return (i ^ 1, j) if j in (0, ny - 1) else (i, far(j))

    return (
        swapped(x_near, lambda i, j: (i ^ 1, j)),
        swapped(x_far, x_far_partner),
        swapped(y_near, lambda i, j: (i, j ^ 1)),
        swapped(y_far, y_far_partner),
    )


def near_far(axis, first, last):
    even = lax.axis_index(axis) % 2 == 0
    return jnp.where(even, last, first), jnp.where(even, first, last)


def before_after(axis, near, far):
    place = lax.axis_index(axis)
    even = place % 2 == 0
    before = jnp.where(place > 0, jnp.where(even, far, near), 0.0)
    after = jnp.where(place < lax.axis_size(axis) - 1, jnp.where(even, near, far), 0.0)
    return before, after


def per_device(source, cell_class, class_conductivity, layer_of_depth, inverses):
    fine = ((6, 8, 16, 128), F32)
    coarse = ((6, 4, 8, 128), F32)
    matrices = ((8, 192, 192), BF16)
    fine_faces = [((6, 16, 128), F32)] * 4
    coarse_faces = [((6, 8, 128), F32)] * 4
    columns = pltpu.VMEM((192, 512), F32)
    coarse_columns = pltpu.VMEM((192, 128), F32)

    x0, b0, high, low, layers, *faces = call(
        first_kernel,
        [fine, fine, matrices, matrices, ((8, 256), jnp.int32)] + fine_faces,
        (source, layer_of_depth.reshape(1, 64), inverses),
        [
            pltpu.VMEM(source.shape, F32),
            pltpu.VMEM((1, 64), jnp.int32),
            pltpu.VMEM(inverses.shape, F32),
            columns,
            pltpu.SemaphoreType.DMA((3,)),
        ],
        spaces=(pltpu.HBM,) * 3,
    )
    halos = exchange(*faces)
    r0, own_b1, sigma0, sigma1 = call(
        own_kernel,
        [fine, coarse, ((8, 16, 128), F32), ((4, 8, 128), F32)],
        (class_conductivity, cell_class, b0, x0),
        [pltpu.VMEM((28, 16, 128), F32)],
        spaces=(pltpu.SMEM, pltpu.VMEM),
    )
    b1, x1a, *faces = call(
        second_kernel,
        [coarse, coarse] + coarse_faces,
        (own_b1, layers, *halos, high, low),
        [pltpu.VMEM((12, 16, 128), F32), coarse_columns],
    )
    fine_halos = halos
    halos = exchange(*faces)
    (y0,) = call(middle_kernel, [fine], (layers, x0, r0, *fine_halos, high, low), [columns])
    x1, *faces = call(
        third_kernel, [coarse] + coarse_faces, (layers, y0, b1, x1a, sigma1, *halos, high, low), [coarse_columns]
    )
    halos = exchange(*faces)
    image, base = call(
        prolong_kernel,
        [fine, fine],
        (x1, sigma0, y0),
        [pltpu.VMEM((6, 4, 8, 128), F32), pltpu.VMEM((6, 4, 16, 128), F32)],
    )
    (out,) = call(
        last_kernel,
        [fine],
        (layers, image, base, *halos, high, low),
        [pltpu.VMEM((12, 16, 128), F32), columns],
        last=True,
    )
    return out


def solution(mesh):
    placed = (P(None, "gx", "gy", None), P("gx", "gy", None), P(), P(), P())
    return jax.shard_map(
        per_device, mesh=mesh, in_specs=placed, out_specs=P(None, "gx", "gy", None), check_vma=False
    )
```

```python
import jax
import jax.numpy as jnp
from jax import lax
from jax.experimental import pallas as pl
from jax.experimental.pallas import tpu as pltpu
from jax.sharding import PartitionSpec as P

damping = 0.8
F32 = jnp.float32
BF16 = jnp.bfloat16


def lane_of(shape):
    return lax.broadcasted_iota(jnp.int32, shape, 1)


def row_of(shape):
    return lax.broadcasted_iota(jnp.int32, shape, 0)


def take_lanes(v, index):
    return jnp.take_along_axis(v, index, axis=1, mode="promise_in_bounds")


def take_rows(v, index):
    return jnp.take_along_axis(v, index, axis=0, mode="promise_in_bounds")


def split_index(shape):
    j = lane_of(shape)
    return ((j & 63) << 1) | (j >> 6)


def join_index(shape):
    j = lane_of(shape)
    return ((j & 1) << 6) | (j >> 1)


class Blocker:
    def __init__(self, half):
        s = row_of((8, 128))
        j = lane_of((8, 128))
        self.half = half
        self.stay = (s < 4) == ((j & (2 * half - 1)) < half)
        self.to = ((s & 1) << 2) | (s >> 1)
        self.back = ((s & 3) << 1) | (s >> 2)

    def swap(self, v):
        return jnp.where(self.stay, v, pltpu.roll(pltpu.roll(v, 4, 0), self.half, 1))

    def forward(self, v):
        return take_rows(self.swap(v), self.to)

    def inverse(self, v):
        return self.swap(take_rows(v, self.back))


def dot(a, b):
    return lax.dot_general(a, b, (((1,), (0,)), ((), ())), preferred_element_type=F32)


def block_product(x, high, low, layer):
    x_high = x.astype(BF16)
    x_low = (x - x_high.astype(F32)).astype(BF16)
    total = jnp.zeros(x.shape, F32)
    for index in range(high.shape[0]):
        part = dot(high[index], x_high) + dot(low[index], x_high) + dot(high[index], x_low)
        total = jnp.where(layer == index, part, total)
    return total


def fine_layers(depth_ref):
    v = depth_ref[...]
    return jnp.concatenate([v] * 8, axis=1)


def coarse_layers(depth_ref):
    v = depth_ref[...]
    v = jnp.broadcast_to(jnp.concatenate([v, v], axis=1), (8, 128))
    return take_lanes(v, (lane_of((8, 128)) & 31) << 1)[0:1]


def fine_columns(blocker, get, put):
    for c in range(6):
        for x in range(8):
            v = get(c, x)
            for t in range(2):
                put(c * 32 + (x % 4) * 8, ((x // 4) * 2 + t) * 128, blocker.forward(v[8 * t : 8 * t + 8]))


def fine_smooth(blocker, columns, high, low, layer, put, finish=lambda bx: None):
    for bx in range(2):
        half = slice(bx * 256, bx * 256 + 256)
        total = block_product(columns[:, half], high, low, layer[:, half]) * damping
        for c in range(6):
            for x in range(4):
                row = c * 32 + x * 8
                for t in range(2):
                    put(c, 4 * bx + x, t, blocker.inverse(total[row : row + 8, 128 * t : 128 * t + 128]))
        finish(bx)


def store_columns(columns):
    def put(row, lane, v):
        columns[row : row + 8, lane : lane + 128] = v

    return put


def coarse_smooth(blocker, columns, get, high, low, layer):
    for c in range(6):
        for x in range(4):
            row = c * 32 + x * 8
            columns[row : row + 8, :] = blocker.forward(get(c, x))
    x = columns[...]
    x_high = x.astype(BF16)
    x_low = (x - x_high.astype(F32)).astype(BF16)
    both = jnp.where(lane_of(x.shape) < 64, x_high.astype(F32), x_low.astype(F32)).astype(BF16)
    total = jnp.zeros(x.shape, F32)
    for index in range(high.shape[0]):
        part = dot(high[index], both) + dot(low[index], both)
        total = jnp.where(layer == index, part, total)
    total = (total + pltpu.roll(total, 64, 1)) * (damping * 4.0)
    return lambda c, x: blocker.inverse(total[c * 32 + x * 8 : c * 32 + x * 8 + 8])


def first_kernel(
    source_hbm, depth_hbm, inverses_hbm, conductivity_hbm, x0, b0, high, low, layers, table, x_near, x_far, y_near, y_far,
    source, depth, inverses, conductivity, columns, done,
):
    copies = [
        pltpu.make_async_copy(source_hbm, source, done.at[0]),
        pltpu.make_async_copy(depth_hbm, depth, done.at[1]),
        pltpu.make_async_copy(inverses_hbm, inverses, done.at[2]),
        pltpu.make_async_copy(conductivity_hbm, conductivity, done.at[3]),
    ]
    for copy in copies:
        copy.start()
    blocker = Blocker(64)
    split = split_index((16, 128))
    copies[0].wait()

    for c in range(6):
        for x in range(8):
            b0[c, x] = take_lanes(source[c, x], split)
    fine_columns(blocker, lambda c, x: b0[c, x], store_columns(columns))
    copies[1].wait()
    layers[0:1, :] = fine_layers(depth)
    layers[1:2, 0:128] = coarse_layers(depth)
    copies[3].wait()
    values = jnp.broadcast_to(conductivity[...], (8, 8))
    own = jnp.where(row_of((8, 8)) == lane_of((8, 8)), values, 0.0)
    table[...] = jnp.broadcast_to(jnp.sum(own, axis=1, keepdims=True), (8, 128))
    copies[2].wait()
    for index in range(8):
        m = inverses[index]
        m_high = m.astype(BF16)
        high[index] = m_high
        low[index] = (m - m_high.astype(F32)).astype(BF16)

    def put(c, x, t, v):
        x0[c, x, 8 * t : 8 * t + 8, :] = v

    fine_smooth(blocker, columns, high, low, layers[0:1, :], put)
    for c in range(6):
        x_near[c], x_far[c] = near_far("gx", x0[c, 0], x0[c, 7])
        y_near[c, 0:8], y_far[c, 0:8] = near_far("gy", x0[c, :, 0, :], x0[c, :, 15, :])
        y_near[c, 8:16] = y_near[c, 0:8]
        y_far[c, 8:16] = y_far[c, 0:8]


def around(u, y_before, y_after, half, other, keep, row):
    size = u.shape[0]
    before = jnp.where(row == 0, y_before, pltpu.roll(u, 1, 0))
    after = jnp.where(row == size - 1, y_after, pltpu.roll(u, size - 1, 0))
    return before + after + pltpu.roll(u, half, 1) + jnp.where(keep, take_lanes(u, other), 0.0)


def fine_other(shape):
    j = lane_of(shape)
    return jnp.where(j < 64, jnp.maximum(j + 63, 64), jnp.minimum(j - 63, 63)), (j != 0) & (j != 127)


def coarse_other(shape):
    j = lane_of(shape) & 63
    return jnp.where(j < 32, jnp.maximum(j + 31, 32), jnp.minimum(j - 31, 31)), (j != 0) & (j != 63)


def pair_index(shape):
    j = lane_of(shape)
    return ((j & 31) << 1) | ((j >> 5) & 1)


def own_kernel(classes, table, b0, x0, r0, b1, sigma0, sigma1, rows, sums):
    shape = (16, 128)
    split = split_index(shape)
    other, keep = fine_other(shape)
    row = row_of(shape)
    pair = pair_index(shape)

    for x in range(8):
        kind = take_lanes(classes[x], split)
        sigma = jnp.zeros(shape, F32)
        for index in range(8):
            sigma = jnp.where(kind == index, table[index : index + 1, :], sigma)
        sigma0[x] = sigma
    for xx in range(4):
        sums[xx * 7 + 6] = sigma0[2 * xx] + sigma0[2 * xx + 1]
        for c in range(3):
            total = {}
            for x in (2 * xx, 2 * xx + 1):
                re = x0[c, x]
                im = x0[c + 3, x]
                sigma = sigma0[x]
                for comp, u, turn in ((c, re, -im), (c + 3, im, re)):
                    beside = around(u, 0.0, 0.0, 64, other, keep, row)
                    if x > 0:
                        beside = beside + x0[comp, x - 1]
                    if x < 7:
                        beside = beside + x0[comp, x + 1]
                    rest = b0[comp, x] - (6.0 * u - beside + sigma * turn)
                    r0[comp, x] = rest
                    total[comp] = rest + total[comp] if comp in total else rest
            for comp in total:
                sums[xx * 7 + comp] = total[comp]
    for slot in range(28):
        v = sums[slot]
        rows[slot] = take_lanes(v + pltpu.roll(v, 64, 1), pair)
    for xx in range(4):
        for c in range(7):
            slot = xx * 7 + c
            v = (rows[slot, pl.ds(0, 8, stride=2), :] + rows[slot, pl.ds(1, 8, stride=2), :]) * 0.125
            if c < 6:
                b1[c, xx] = v
            else:
                sigma1[xx] = v


def second_kernel(
    own_b1, layers, x_near_in, x_far_in, y_near_in, y_far_in, high, low,
    b1, x1, x_near, x_far, y_near, y_far, rows, columns,
):
    shape = (16, 128)
    pair = pair_index(shape)
    narrow = (8, 128)
    row = row_of(narrow)
    for c in range(6):
        added = []
        for side, v in enumerate(before_after("gx", x_near_in[c], x_far_in[c])):
            slot = 2 * c + side
            rows[slot] = take_lanes(v + pltpu.roll(v, 64, 1), pair)
            added.append((rows[slot, pl.ds(0, 8, stride=2), :] + rows[slot, pl.ds(1, 8, stride=2), :]) * 0.125)
        edges = []
        for v in before_after("gy", y_near_in[c, 0:8], y_far_in[c, 0:8]):
            v = take_lanes(v + pltpu.roll(v, 64, 1), pair[0:8])
            edges.append((v + pltpu.roll(v, 7, 0)) * 0.125)
        for x in range(4):
            v = own_b1[c, x] + jnp.where(row == 0, edges[0][2 * x : 2 * x + 1], 0.0)
            v = v + jnp.where(row == 7, edges[1][2 * x : 2 * x + 1], 0.0)
            if x == 0:
                v = v + added[0]
            if x == 3:
                v = v + added[1]
            b1[c, x] = v
    result = coarse_smooth(Blocker(32), columns, lambda c, x: b1[c, x], high, low, layers[1:2, 0:128])
    store_coarse(result, x1, x_near, x_far, y_near, y_far)


def store_coarse(result, x1, x_near, x_far, y_near, y_far):
    for c in range(6):
        for x in range(4):
            x1[c, x] = result(c, x)
        x_near[c], x_far[c] = near_far("gx", x1[c, 0], x1[c, 3])
        y_near[c, 0:4], y_far[c, 0:4] = near_far("gy", x1[c, :, 0, :], x1[c, :, 7, :])
        y_near[c, 4:8] = y_near[c, 0:4]
        y_far[c, 4:8] = y_far[c, 0:4]


def middle_kernel(layers, x0, r0, x_near_in, x_far_in, y_near_in, y_far_in, high, low, y0, columns):
    blocker = Blocker(64)
    row = row_of((16, 128))
    x_halo = [before_after("gx", x_near_in[c], x_far_in[c]) for c in range(6)]
    y_halo = [before_after("gy", y_near_in[c, 0:8], y_far_in[c, 0:8]) for c in range(6)]

    def get(c, x):
        v = r0[c, x] + jnp.where(row == 0, y_halo[c][0][x : x + 1], 0.0)
        v = v + jnp.where(row == 15, y_halo[c][1][x : x + 1], 0.0)
        if x == 0:
            v = v + x_halo[c][0]
        if x == 7:
            v = v + x_halo[c][1]
        return v

    fine_columns(blocker, get, store_columns(columns))

    def put(c, x, t, v):
        y0[c, x, 8 * t : 8 * t + 8, :] = x0[c, x, 8 * t : 8 * t + 8, :] + v

    fine_smooth(blocker, columns, high, low, layers[0:1, :], put)


def third_kernel(
    layers, y0, b1, x1a, sigma1, x_near_in, x_far_in, y_near_in, y_far_in, high, low,
    x1, x_near, x_far, y_near, y_far, columns,
):
    x_halo = [before_after("gx", x_near_in[c], x_far_in[c]) for c in range(6)]
    y_halo = [before_after("gy", y_near_in[c], y_far_in[c]) for c in range(6)]
    shape = (8, 128)
    other, keep = coarse_other(shape)
    row = row_of(shape)

    def residual(c, x):
        u = x1a[c, x]
        turn = -x1a[c + 3, x] if c < 3 else x1a[c - 3, x]
        beside = around(u, y_halo[c][0][x : x + 1], y_halo[c][1][x : x + 1], 32, other, keep, row)
        beside = beside + (x1a[c, x - 1] if x > 0 else x_halo[c][0])
        beside = beside + (x1a[c, x + 1] if x < 3 else x_halo[c][1])
        return b1[c, x] - ((6.0 * u - beside) * 0.25 + sigma1[x] * turn)

    more = coarse_smooth(Blocker(32), columns, residual, high, low, layers[1:2, 0:128])
    store_coarse(lambda c, x: x1a[c, x] + more(c, x), x1, x_near, x_far, y_near, y_far)


def self_index(shape):
    k = lane_of(shape) & 63
    return ((k & 1) << 5) | (k >> 1)


def prolong_kernel(x1, sigma0, y0, image, base, coarse, rows):
    shape = (8, 128)
    j = lane_of(shape)
    row = row_of(shape)
    k = j & 63
    beyond = jnp.where(j < 64, k - 1, k + 1)
    inside = (beyond >= 0) & (beyond < 64)
    beyond = jnp.clip(beyond, 0, 63)
    next_index = ((beyond & 1) << 5) | (beyond >> 1)
    own_index = self_index(shape)

    for c in range(6):
        for x in range(4):
            coarse[c, x] = take_lanes(x1[c, x], own_index)
    for xx in range(4):
        for c in range(3):
            own = {}
            for comp in (c, c + 3):
                v = coarse[comp, xx]
                beside = jnp.where(inside, take_lanes(x1[comp, xx], next_index), 0.0)
                before = jnp.where(row == 0, 0.0, pltpu.roll(v, 1, 0))
                after = jnp.where(row == 7, 0.0, pltpu.roll(v, 7, 0))
                own[comp] = (v, 3.0 * v - beside, before, after)
                rows[comp, xx, pl.ds(0, 8, stride=2), :] = v
                rows[comp, xx, pl.ds(1, 8, stride=2), :] = v
            for half in range(2):
                x = 2 * xx + half
                next_x = xx - 1 + 2 * half
                for parity in range(2):
                    sigma = sigma0[x, pl.ds(parity, 8, stride=2), :]
                    for comp, partner, sign in ((c, c + 3, -1.0), (c + 3, c, 1.0)):
                        v, kept, before, after = own[comp]
                        value = kept - (before, after)[parity] + sign * sigma * own[partner][0]
                        if 0 <= next_x < 4:
                            value = value - coarse[comp, next_x]
                        image[comp, x, pl.ds(parity, 8, stride=2), :] = value
                for comp in (c, c + 3):
                    base[comp, x] = y0[comp, x] + rows[comp, xx]


def last_kernel(layers, image, base, x_near_in, x_far_in, y_near_in, y_far_in, high, low, out, rows, columns, stage, done):
    shape = (8, 128)
    own_index = self_index(shape)
    row = row_of((16, 128))
    y_halo = []
    for c in range(6):
        for side, v in enumerate(before_after("gx", x_near_in[c], x_far_in[c])):
            v = take_lanes(v, own_index)
            slot = 2 * c + side
            rows[slot, pl.ds(0, 8, stride=2), :] = v
            rows[slot, pl.ds(1, 8, stride=2), :] = v
        y_halo.append([take_lanes(v, own_index) for v in before_after("gy", y_near_in[c], y_far_in[c])])

    def get(c, x):
        v = image[c, x] - jnp.where(row == 0, y_halo[c][0][x // 2 : x // 2 + 1], 0.0)
        v = v - jnp.where(row == 15, y_halo[c][1][x // 2 : x // 2 + 1], 0.0)
        if x == 0:
            v = v - rows[2 * c]
        if x == 7:
            v = v - rows[2 * c + 1]
        return v

    blocker = Blocker(64)
    fine_columns(blocker, get, store_columns(columns))
    join = join_index((16, 128))
    copies = []

    def put(c, x, t, v):
        stage[c, x, 8 * t : 8 * t + 8, :] = base[c, x, 8 * t : 8 * t + 8, :] - v

    def finish(bx):
        for c in range(6):
            for x in range(4 * bx, 4 * bx + 4):
                stage[c, x] = take_lanes(stage[c, x], join)
        part = pl.ds(4 * bx, 4)
        copies.append(pltpu.make_async_copy(stage.at[:, part], out.at[:, part], done.at[bx]))
        copies[bx].start()

    fine_smooth(blocker, columns, high, low, layers[0:1, :], put, finish)
    for copy in copies:
        copy.wait()


def call(kernel, outs, args, scratch, spaces=(), last=False):
    vmem = pl.BlockSpec(memory_space=pltpu.VMEM)
    own = len(spaces)
    args = [pltpu.with_memory_space_constraint(arg, space) for arg, space in zip(args, spaces)] + [pltpu.with_memory_space_constraint(arg, pltpu.VMEM) for arg in args[own:]]
    return pl.pallas_call(
        kernel,
        out_shape=[jax.ShapeDtypeStruct(*out) if last else pltpu.VMEM(*out) for out in outs],
        in_specs=[pl.BlockSpec(memory_space=space) for space in spaces] + [vmem] * (len(args) - own),
        out_specs=[pl.BlockSpec(memory_space=pltpu.HBM) if last else vmem] * len(outs),
        scratch_shapes=scratch,
        compiler_params=pltpu.CompilerParams(vmem_limit_bytes=12 << 20),
        name=kernel.__name__,
    )(*args)


def exchange(x_near, x_far, y_near, y_far):
    nx, ny = lax.axis_size("gx"), lax.axis_size("gy")

    def swapped(array, partner):
        pairs = [(i * ny + j, partner(i, j)) for i in range(nx) for j in range(ny)]
        return lax.ppermute(array, ("gx", "gy"), [(a, i * ny + j) for a, (i, j) in pairs])

    def far(i):
        return i + 1 if i % 2 else i - 1

    def x_far_partner(i, j):
        return (i, j ^ 1) if i in (0, nx - 1) else (far(i), j)

    def y_far_partner(i, j):
        return (i ^ 1, j) if j in (0, ny - 1) else (i, far(j))

    return (
        swapped(x_near, lambda i, j: (i ^ 1, j)),
        swapped(x_far, x_far_partner),
        swapped(y_near, lambda i, j: (i, j ^ 1)),
        swapped(y_far, y_far_partner),
    )


def near_far(axis, first, last):
    even = lax.axis_index(axis) % 2 == 0
    return jnp.where(even, last, first), jnp.where(even, first, last)


def before_after(axis, near, far):
    place = lax.axis_index(axis)
    even = place % 2 == 0
    before = jnp.where(place > 0, jnp.where(even, far, near), 0.0)
    after = jnp.where(place < lax.axis_size(axis) - 1, jnp.where(even, near, far), 0.0)
    return before, after


def per_device(source, cell_class, class_conductivity, layer_of_depth, inverses):
    fine = ((6, 8, 16, 128), F32)
    coarse = ((6, 4, 8, 128), F32)
    matrices = ((8, 192, 192), BF16)
    fine_faces = [((6, 16, 128), F32)] * 4
    coarse_faces = [((6, 8, 128), F32)] * 4
    columns = pltpu.VMEM((192, 512), F32)
    coarse_columns = pltpu.VMEM((192, 128), F32)

    x0, b0, high, low, layers, table, *faces = call(
        first_kernel,
        [fine, fine, matrices, matrices, ((8, 512), jnp.int32), ((8, 128), F32)] + fine_faces,
        (source, layer_of_depth.reshape(1, 64), inverses, class_conductivity.reshape(1, 8)),
        [
            pltpu.VMEM(source.shape, F32),
            pltpu.VMEM((1, 64), jnp.int32),
            pltpu.VMEM(inverses.shape, F32),
            pltpu.VMEM((1, 8), F32),
            columns,
            pltpu.SemaphoreType.DMA((4,)),
        ],
        spaces=(pltpu.HBM,) * 4,
    )
    halos = exchange(*faces)
    r0, own_b1, sigma0, sigma1 = call(
        own_kernel,
        [fine, coarse, ((8, 16, 128), F32), ((4, 8, 128), F32)],
        (cell_class, table, b0, x0),
        [pltpu.VMEM((28, 16, 128), F32)] * 2,
        spaces=(pltpu.VMEM,),
    )
    b1, x1a, *faces = call(
        second_kernel,
        [coarse, coarse] + coarse_faces,
        (own_b1, layers, *halos, high, low),
        [pltpu.VMEM((12, 16, 128), F32), coarse_columns],
    )
    fine_halos = halos
    halos = exchange(*faces)
    (y0,) = call(middle_kernel, [fine], (layers, x0, r0, *fine_halos, high, low), [columns])
    x1, *faces = call(
        third_kernel, [coarse] + coarse_faces, (layers, y0, b1, x1a, sigma1, *halos, high, low), [coarse_columns]
    )
    halos = exchange(*faces)
    image, base = call(
        prolong_kernel,
        [fine, fine],
        (x1, sigma0, y0),
        [pltpu.VMEM((6, 4, 8, 128), F32), pltpu.VMEM((6, 4, 16, 128), F32)],
    )
    (out,) = call(
        last_kernel,
        [fine],
        (layers, image, base, *halos, high, low),
        [pltpu.VMEM((12, 16, 128), F32), columns, pltpu.VMEM(*fine), pltpu.SemaphoreType.DMA((2,))],
        last=True,
    )
    return out


def solution(mesh):
    placed = (P(None, "gx", "gy", None), P("gx", "gy", None), P(), P(), P())
    return jax.shard_map(
        per_device, mesh=mesh, in_specs=placed, out_specs=P(None, "gx", "gy", None), check_vma=False
    )
```

```python
import jax
import jax.numpy as jnp
from jax import lax
from jax.experimental import pallas as pl
from jax.experimental.pallas import tpu as pltpu
from jax.sharding import PartitionSpec as P

damping = 0.8
F32 = jnp.float32
BF16 = jnp.bfloat16


def lane_of(shape):
    return lax.broadcasted_iota(jnp.int32, shape, 1)


def row_of(shape):
    return lax.broadcasted_iota(jnp.int32, shape, 0)


def take_lanes(v, index):
    return jnp.take_along_axis(v, index, axis=1, mode="promise_in_bounds")


def take_rows(v, index):
    return jnp.take_along_axis(v, index, axis=0, mode="promise_in_bounds")


def split_index(shape):
    j = lane_of(shape)
    return ((j & 63) << 1) | (j >> 6)


def join_index(shape):
    j = lane_of(shape)
    return ((j & 1) << 6) | (j >> 1)


class Blocker:
    def __init__(self, half):
        s = row_of((8, 128))
        j = lane_of((8, 128))
        self.half = half
        self.stay = (s < 4) == ((j & (2 * half - 1)) < half)
        self.to = ((s & 1) << 2) | (s >> 1)
        self.back = ((s & 3) << 1) | (s >> 2)

    def swap(self, v):
        return jnp.where(self.stay, v, pltpu.roll(pltpu.roll(v, 4, 0), self.half, 1))

    def forward(self, v):
        return take_rows(self.swap(v), self.to)

    def inverse(self, v):
        return self.swap(take_rows(v, self.back))


def dot(a, b):
    return lax.dot_general(a, b, (((1,), (0,)), ((), ())), preferred_element_type=F32)


def block_product(x, high, low, layer):
    x_high = x.astype(BF16)
    x_low = (x - x_high.astype(F32)).astype(BF16)
    total = jnp.zeros(x.shape, F32)
    for index in range(high.shape[0]):
        part = dot(high[index], x_high) + dot(low[index], x_high) + dot(high[index], x_low)
        total = jnp.where(layer == index, part, total)
    return total


def fine_layers(depth_ref):
    v = depth_ref[...]
    return jnp.concatenate([v] * 8, axis=1)


def coarse_layers(depth_ref):
    v = depth_ref[...]
    v = jnp.broadcast_to(jnp.concatenate([v, v], axis=1), (8, 128))
    return take_lanes(v, (lane_of((8, 128)) & 31) << 1)[0:1]


def fine_columns(blocker, get, put):
    for c in range(6):
        for x in range(8):
            v = get(c, x)
            for t in range(2):
                put(c * 32 + (x % 4) * 8, ((x // 4) * 2 + t) * 128, blocker.forward(v[8 * t : 8 * t + 8]))


def fine_smooth(blocker, columns, high, low, layer, put, finish=lambda bx: None):
    for bx in range(2):
        half = slice(bx * 256, bx * 256 + 256)
        total = block_product(columns[:, half], high, low, layer[:, half]) * damping
        for c in range(6):
            for x in range(4):
                row = c * 32 + x * 8
                for t in range(2):
                    put(c, 4 * bx + x, t, blocker.inverse(total[row : row + 8, 128 * t : 128 * t + 128]))
        finish(bx)


def store_columns(columns):
    def put(row, lane, v):
        columns[row : row + 8, lane : lane + 128] = v

    return put


def coarse_smooth(blocker, columns, get, high, low, layer):
    for c in range(6):
        for x in range(4):
            row = c * 32 + x * 8
            columns[row : row + 8, :] = blocker.forward(get(c, x))
    x = columns[...]
    x_high = x.astype(BF16)
    x_low = (x - x_high.astype(F32)).astype(BF16)
    both = jnp.where(lane_of(x.shape) < 64, x_high.astype(F32), x_low.astype(F32)).astype(BF16)
    total = jnp.zeros(x.shape, F32)
    for index in range(high.shape[0]):
        part = dot(high[index], both) + dot(low[index], both)
        total = jnp.where(layer == index, part, total)
    total = (total + pltpu.roll(total, 64, 1)) * (damping * 4.0)
    return lambda c, x: blocker.inverse(total[c * 32 + x * 8 : c * 32 + x * 8 + 8])


def first_kernel(
    source_hbm, depth_hbm, inverses_hbm, conductivity_hbm, x0, b0, high, low, layers, table, x_far, x_near, y_far, y_near,
    source, depth, inverses, conductivity, columns, done,
):
    copies = [
        pltpu.make_async_copy(source_hbm, source, done.at[0]),
        pltpu.make_async_copy(depth_hbm, depth, done.at[1]),
        pltpu.make_async_copy(inverses_hbm, inverses, done.at[2]),
        pltpu.make_async_copy(conductivity_hbm, conductivity, done.at[3]),
    ]
    for copy in copies:
        copy.start()
    blocker = Blocker(64)
    split = split_index((16, 128))
    copies[0].wait()

    for c in range(6):
        for x in range(8):
            b0[c, x] = take_lanes(source[c, x], split)
    fine_columns(blocker, lambda c, x: b0[c, x], store_columns(columns))
    copies[1].wait()
    layers[0:1, :] = fine_layers(depth)
    layers[1:2, 0:128] = coarse_layers(depth)
    copies[3].wait()
    values = jnp.broadcast_to(conductivity[...], (8, 8))
    own = jnp.where(row_of((8, 8)) == lane_of((8, 8)), values, 0.0)
    table[...] = jnp.broadcast_to(jnp.sum(own, axis=1, keepdims=True), (8, 128))
    copies[2].wait()
    for index in range(8):
        m = inverses[index]
        m_high = m.astype(BF16)
        high[index] = m_high
        low[index] = (m - m_high.astype(F32)).astype(BF16)

    def put(c, x, t, v):
        x0[c, x, 8 * t : 8 * t + 8, :] = v

    fine_smooth(blocker, columns, high, low, layers[0:1, :], put)
    for c in range(6):
        x_near[c], x_far[c] = near_far("gx", x0[c, 0], x0[c, 7])
        y_near[c, 0:8], y_far[c, 0:8] = near_far("gy", x0[c, :, 0, :], x0[c, :, 15, :])
        y_near[c, 8:16] = y_near[c, 0:8]
        y_far[c, 8:16] = y_far[c, 0:8]


def around(u, y_before, y_after, half, other, keep, row):
    size = u.shape[0]
    before = jnp.where(row == 0, y_before, pltpu.roll(u, 1, 0))
    after = jnp.where(row == size - 1, y_after, pltpu.roll(u, size - 1, 0))
    return before + after + pltpu.roll(u, half, 1) + jnp.where(keep, take_lanes(u, other), 0.0)


def fine_other(shape):
    j = lane_of(shape)
    return jnp.where(j < 64, jnp.maximum(j + 63, 64), jnp.minimum(j - 63, 63)), (j != 0) & (j != 127)


def coarse_other(shape):
    j = lane_of(shape) & 63
    return jnp.where(j < 32, jnp.maximum(j + 31, 32), jnp.minimum(j - 31, 31)), (j != 0) & (j != 63)


def pair_index(shape):
    j = lane_of(shape)
    return ((j & 31) << 1) | ((j >> 5) & 1)


def own_kernel(classes, table, b0, x0, r0, b1, sigma0, sigma1, rows, sums):
    shape = (16, 128)
    split = split_index(shape)
    other, keep = fine_other(shape)
    row = row_of(shape)
    pair = pair_index(shape)

    for x in range(8):
        kind = take_lanes(classes[x], split)
        sigma = jnp.zeros(shape, F32)
        for index in range(8):
            sigma = jnp.where(kind == index, table[index : index + 1, :], sigma)
        sigma0[x] = sigma
    for xx in range(4):
        sums[xx * 7 + 6] = sigma0[2 * xx] + sigma0[2 * xx + 1]
        for c in range(3):
            total = {}
            for x in (2 * xx, 2 * xx + 1):
                re = x0[c, x]
                im = x0[c + 3, x]
                sigma = sigma0[x]
                for comp, u, turn in ((c, re, -im), (c + 3, im, re)):
                    beside = around(u, 0.0, 0.0, 64, other, keep, row)
                    if x > 0:
                        beside = beside + x0[comp, x - 1]
                    if x < 7:
                        beside = beside + x0[comp, x + 1]
                    rest = b0[comp, x] - (6.0 * u - beside + sigma * turn)
                    r0[comp, x] = rest
                    total[comp] = rest + total[comp] if comp in total else rest
            for comp in total:
                sums[xx * 7 + comp] = total[comp]
    for slot in range(28):
        v = sums[slot]
        rows[slot] = take_lanes(v + pltpu.roll(v, 64, 1), pair)
    for xx in range(4):
        for c in range(7):
            slot = xx * 7 + c
            v = (rows[slot, pl.ds(0, 8, stride=2), :] + rows[slot, pl.ds(1, 8, stride=2), :]) * 0.125
            if c < 6:
                b1[c, xx] = v
            else:
                sigma1[xx] = v


def second_kernel(
    own_b1, layers, x_far_in, x_near_in, y_far_in, y_near_in, high, low,
    b1, x1, x_far, x_near, y_far, y_near, rows, columns,
):
    shape = (16, 128)
    pair = pair_index(shape)
    narrow = (8, 128)
    row = row_of(narrow)
    for c in range(6):
        added = []
        for side, v in enumerate(before_after("gx", x_near_in[c], x_far_in[c])):
            slot = 2 * c + side
            rows[slot] = take_lanes(v + pltpu.roll(v, 64, 1), pair)
            added.append((rows[slot, pl.ds(0, 8, stride=2), :] + rows[slot, pl.ds(1, 8, stride=2), :]) * 0.125)
        edges = []
        for v in before_after("gy", y_near_in[c, 0:8], y_far_in[c, 0:8]):
            v = take_lanes(v + pltpu.roll(v, 64, 1), pair[0:8])
            edges.append((v + pltpu.roll(v, 7, 0)) * 0.125)
        for x in range(4):
            v = own_b1[c, x] + jnp.where(row == 0, edges[0][2 * x : 2 * x + 1], 0.0)
            v = v + jnp.where(row == 7, edges[1][2 * x : 2 * x + 1], 0.0)
            if x == 0:
                v = v + added[0]
            if x == 3:
                v = v + added[1]
            b1[c, x] = v
    result = coarse_smooth(Blocker(32), columns, lambda c, x: b1[c, x], high, low, layers[1:2, 0:128])
    store_coarse(result, x1, x_far, x_near, y_far, y_near)


def store_coarse(result, x1, x_far, x_near, y_far, y_near):
    for c in range(6):
        for x in range(4):
            x1[c, x] = result(c, x)
        x_near[c], x_far[c] = near_far("gx", x1[c, 0], x1[c, 3])
        y_near[c, 0:4], y_far[c, 0:4] = near_far("gy", x1[c, :, 0, :], x1[c, :, 7, :])
        y_near[c, 4:8] = y_near[c, 0:4]
        y_far[c, 4:8] = y_far[c, 0:4]


def middle_kernel(layers, x0, r0, x_far_in, x_near_in, y_far_in, y_near_in, high, low, y0, columns):
    blocker = Blocker(64)
    row = row_of((16, 128))
    x_halo = [before_after("gx", x_near_in[c], x_far_in[c]) for c in range(6)]
    y_halo = [before_after("gy", y_near_in[c, 0:8], y_far_in[c, 0:8]) for c in range(6)]

    def get(c, x):
        v = r0[c, x] + jnp.where(row == 0, y_halo[c][0][x : x + 1], 0.0)
        v = v + jnp.where(row == 15, y_halo[c][1][x : x + 1], 0.0)
        if x == 0:
            v = v + x_halo[c][0]
        if x == 7:
            v = v + x_halo[c][1]
        return v

    fine_columns(blocker, get, store_columns(columns))

    def put(c, x, t, v):
        y0[c, x, 8 * t : 8 * t + 8, :] = x0[c, x, 8 * t : 8 * t + 8, :] + v

    fine_smooth(blocker, columns, high, low, layers[0:1, :], put)


def third_kernel(
    layers, y0, b1, x1a, sigma1, x_far_in, x_near_in, y_far_in, y_near_in, high, low,
    x1, x_far, x_near, y_far, y_near, columns,
):
    x_halo = [before_after("gx", x_near_in[c], x_far_in[c]) for c in range(6)]
    y_halo = [before_after("gy", y_near_in[c], y_far_in[c]) for c in range(6)]
    shape = (8, 128)
    other, keep = coarse_other(shape)
    row = row_of(shape)

    def residual(c, x):
        u = x1a[c, x]
        turn = -x1a[c + 3, x] if c < 3 else x1a[c - 3, x]
        beside = around(u, y_halo[c][0][x : x + 1], y_halo[c][1][x : x + 1], 32, other, keep, row)
        beside = beside + (x1a[c, x - 1] if x > 0 else x_halo[c][0])
        beside = beside + (x1a[c, x + 1] if x < 3 else x_halo[c][1])
        return b1[c, x] - ((6.0 * u - beside) * 0.25 + sigma1[x] * turn)

    more = coarse_smooth(Blocker(32), columns, residual, high, low, layers[1:2, 0:128])
    store_coarse(lambda c, x: x1a[c, x] + more(c, x), x1, x_far, x_near, y_far, y_near)


def self_index(shape):
    k = lane_of(shape) & 63
    return ((k & 1) << 5) | (k >> 1)


def prolong_kernel(x1, sigma0, y0, image, base, coarse, rows):
    shape = (8, 128)
    j = lane_of(shape)
    row = row_of(shape)
    k = j & 63
    beyond = jnp.where(j < 64, k - 1, k + 1)
    inside = (beyond >= 0) & (beyond < 64)
    beyond = jnp.clip(beyond, 0, 63)
    next_index = ((beyond & 1) << 5) | (beyond >> 1)
    own_index = self_index(shape)

    for c in range(6):
        for x in range(4):
            coarse[c, x] = take_lanes(x1[c, x], own_index)
    for xx in range(4):
        for c in range(3):
            own = {}
            for comp in (c, c + 3):
                v = coarse[comp, xx]
                beside = jnp.where(inside, take_lanes(x1[comp, xx], next_index), 0.0)
                before = jnp.where(row == 0, 0.0, pltpu.roll(v, 1, 0))
                after = jnp.where(row == 7, 0.0, pltpu.roll(v, 7, 0))
                own[comp] = (v, 3.0 * v - beside, before, after)
                rows[comp, xx, pl.ds(0, 8, stride=2), :] = v
                rows[comp, xx, pl.ds(1, 8, stride=2), :] = v
            for half in range(2):
                x = 2 * xx + half
                next_x = xx - 1 + 2 * half
                for parity in range(2):
                    sigma = sigma0[x, pl.ds(parity, 8, stride=2), :]
                    for comp, partner, sign in ((c, c + 3, -1.0), (c + 3, c, 1.0)):
                        v, kept, before, after = own[comp]
                        value = kept - (before, after)[parity] + sign * sigma * own[partner][0]
                        if 0 <= next_x < 4:
                            value = value - coarse[comp, next_x]
                        image[comp, x, pl.ds(parity, 8, stride=2), :] = value
                for comp in (c, c + 3):
                    base[comp, x] = y0[comp, x] + rows[comp, xx]


def last_kernel(layers, image, base, x_far_in, x_near_in, y_far_in, y_near_in, high, low, out, rows, columns, stage, done):
    shape = (8, 128)
    own_index = self_index(shape)
    row = row_of((16, 128))
    y_halo = []
    for c in range(6):
        for side, v in enumerate(before_after("gx", x_near_in[c], x_far_in[c])):
            v = take_lanes(v, own_index)
            slot = 2 * c + side
            rows[slot, pl.ds(0, 8, stride=2), :] = v
            rows[slot, pl.ds(1, 8, stride=2), :] = v
        y_halo.append([take_lanes(v, own_index) for v in before_after("gy", y_near_in[c], y_far_in[c])])

    def get(c, x):
        v = image[c, x] - jnp.where(row == 0, y_halo[c][0][x // 2 : x // 2 + 1], 0.0)
        v = v - jnp.where(row == 15, y_halo[c][1][x // 2 : x // 2 + 1], 0.0)
        if x == 0:
            v = v - rows[2 * c]
        if x == 7:
            v = v - rows[2 * c + 1]
        return v

    blocker = Blocker(64)
    fine_columns(blocker, get, store_columns(columns))
    join = join_index((16, 128))
    copies = []

    def put(c, x, t, v):
        stage[c, x, 8 * t : 8 * t + 8, :] = base[c, x, 8 * t : 8 * t + 8, :] - v

    def finish(bx):
        for c in range(6):
            for x in range(4 * bx, 4 * bx + 4):
                stage[c, x] = take_lanes(stage[c, x], join)
        part = pl.ds(4 * bx, 4)
        copies.append(pltpu.make_async_copy(stage.at[:, part], out.at[:, part], done.at[bx]))
        copies[bx].start()

    fine_smooth(blocker, columns, high, low, layers[0:1, :], put, finish)
    for copy in copies:
        copy.wait()


def call(kernel, outs, args, scratch, spaces=(), last=False):
    vmem = pl.BlockSpec(memory_space=pltpu.VMEM)
    own = len(spaces)
    args = [pltpu.with_memory_space_constraint(arg, space) for arg, space in zip(args, spaces)] + [pltpu.with_memory_space_constraint(arg, pltpu.VMEM) for arg in args[own:]]
    return pl.pallas_call(
        kernel,
        out_shape=[jax.ShapeDtypeStruct(*out) if last else pltpu.VMEM(*out) for out in outs],
        in_specs=[pl.BlockSpec(memory_space=space) for space in spaces] + [vmem] * (len(args) - own),
        out_specs=[pl.BlockSpec(memory_space=pltpu.HBM) if last else vmem] * len(outs),
        scratch_shapes=scratch,
        compiler_params=pltpu.CompilerParams(vmem_limit_bytes=12 << 20),
        name=kernel.__name__,
    )(*args)


def exchange(x_far, x_near, y_far, y_near):
    nx, ny = lax.axis_size("gx"), lax.axis_size("gy")

    def swapped(array, partner):
        pairs = [(i * ny + j, partner(i, j)) for i in range(nx) for j in range(ny)]
        return lax.ppermute(array, ("gx", "gy"), [(a, i * ny + j) for a, (i, j) in pairs])

    def far(i):
        return i + 1 if i % 2 else i - 1

    def x_far_partner(i, j):
        return (i, j ^ 1) if i in (0, nx - 1) else (far(i), j)

    def y_far_partner(i, j):
        return (i ^ 1, j) if j in (0, ny - 1) else (i, far(j))

    return (
        swapped(x_far, x_far_partner),
        swapped(x_near, lambda i, j: (i ^ 1, j)),
        swapped(y_far, y_far_partner),
        swapped(y_near, lambda i, j: (i, j ^ 1)),
    )


def near_far(axis, first, last):
    even = lax.axis_index(axis) % 2 == 0
    return jnp.where(even, last, first), jnp.where(even, first, last)


def before_after(axis, near, far):
    place = lax.axis_index(axis)
    even = place % 2 == 0
    before = jnp.where(place > 0, jnp.where(even, far, near), 0.0)
    after = jnp.where(place < lax.axis_size(axis) - 1, jnp.where(even, near, far), 0.0)
    return before, after


def per_device(source, cell_class, class_conductivity, layer_of_depth, inverses):
    fine = ((6, 8, 16, 128), F32)
    coarse = ((6, 4, 8, 128), F32)
    matrices = ((8, 192, 192), BF16)
    fine_faces = [((6, 16, 128), F32)] * 4
    coarse_faces = [((6, 8, 128), F32)] * 4
    columns = pltpu.VMEM((192, 512), F32)
    coarse_columns = pltpu.VMEM((192, 128), F32)

    x0, b0, high, low, layers, table, *faces = call(
        first_kernel,
        [fine, fine, matrices, matrices, ((8, 512), jnp.int32), ((8, 128), F32)] + fine_faces,
        (source, layer_of_depth.reshape(1, 64), inverses, class_conductivity.reshape(1, 8)),
        [
            pltpu.VMEM(source.shape, F32),
            pltpu.VMEM((1, 64), jnp.int32),
            pltpu.VMEM(inverses.shape, F32),
            pltpu.VMEM((1, 8), F32),
            columns,
            pltpu.SemaphoreType.DMA((4,)),
        ],
        spaces=(pltpu.HBM,) * 4,
    )
    halos = exchange(*faces)
    r0, own_b1, sigma0, sigma1 = call(
        own_kernel,
        [fine, coarse, ((8, 16, 128), F32), ((4, 8, 128), F32)],
        (cell_class, table, b0, x0),
        [pltpu.VMEM((28, 16, 128), F32)] * 2,
        spaces=(pltpu.VMEM,),
    )
    b1, x1a, *faces = call(
        second_kernel,
        [coarse, coarse] + coarse_faces,
        (own_b1, layers, *halos, high, low),
        [pltpu.VMEM((12, 16, 128), F32), coarse_columns],
    )
    fine_halos = halos
    halos = exchange(*faces)
    (y0,) = call(middle_kernel, [fine], (layers, x0, r0, *fine_halos, high, low), [columns])
    x1, *faces = call(
        third_kernel, [coarse] + coarse_faces, (layers, y0, b1, x1a, sigma1, *halos, high, low), [coarse_columns]
    )
    halos = exchange(*faces)
    image, base = call(
        prolong_kernel,
        [fine, fine],
        (x1, sigma0, y0),
        [pltpu.VMEM((6, 4, 8, 128), F32), pltpu.VMEM((6, 4, 16, 128), F32)],
    )
    (out,) = call(
        last_kernel,
        [fine],
        (layers, image, base, *halos, high, low),
        [pltpu.VMEM((12, 16, 128), F32), columns, pltpu.VMEM(*fine), pltpu.SemaphoreType.DMA((2,))],
        last=True,
    )
    return out


def solution(mesh):
    placed = (P(None, "gx", "gy", None), P("gx", "gy", None), P(), P(), P())
    return jax.shard_map(
        per_device, mesh=mesh, in_specs=placed, out_specs=P(None, "gx", "gy", None), check_vma=False
    )
```

```python
import jax
import jax.numpy as jnp
from jax import lax
from jax.experimental import pallas as pl
from jax.experimental.pallas import tpu as pltpu
from jax.sharding import PartitionSpec as P

damping = 0.8
F32 = jnp.float32
BF16 = jnp.bfloat16


def lane_of(shape):
    return lax.broadcasted_iota(jnp.int32, shape, 1)


def row_of(shape):
    return lax.broadcasted_iota(jnp.int32, shape, 0)


def take_lanes(v, index):
    return jnp.take_along_axis(v, index, axis=1, mode="promise_in_bounds")


def take_rows(v, index):
    return jnp.take_along_axis(v, index, axis=0, mode="promise_in_bounds")


def split_index(shape):
    j = lane_of(shape)
    return ((j & 63) << 1) | (j >> 6)


def join_index(shape):
    j = lane_of(shape)
    return ((j & 1) << 6) | (j >> 1)


class Blocker:
    def __init__(self, half):
        s = row_of((8, 128))
        j = lane_of((8, 128))
        self.half = half
        self.stay = (s < 4) == ((j & (2 * half - 1)) < half)
        self.to = ((s & 1) << 2) | (s >> 1)
        self.back = ((s & 3) << 1) | (s >> 2)

    def swap(self, v):
        return jnp.where(self.stay, v, pltpu.roll(pltpu.roll(v, 4, 0), self.half, 1))

    def forward(self, v):
        return take_rows(self.swap(v), self.to)

    def inverse(self, v):
        return self.swap(take_rows(v, self.back))


def dot(a, b):
    return lax.dot_general(a, b, (((1,), (0,)), ((), ())), preferred_element_type=F32)


def block_product(x, high, low, layer):
    x_high = x.astype(BF16)
    x_low = (x - x_high.astype(F32)).astype(BF16)
    total = jnp.zeros(x.shape, F32)
    for index in range(high.shape[0]):
        part = dot(high[index], x_high) + dot(low[index], x_high) + dot(high[index], x_low)
        total = jnp.where(layer == index, part, total)
    return total


def fine_layers(depth_ref):
    v = depth_ref[...]
    return jnp.concatenate([v] * 8, axis=1)


def coarse_layers(depth_ref):
    v = depth_ref[...]
    v = jnp.broadcast_to(jnp.concatenate([v, v], axis=1), (8, 128))
    return take_lanes(v, (lane_of((8, 128)) & 31) << 1)[0:1]


def fine_columns(blocker, get, put):
    for c in range(6):
        for x in range(8):
            v = get(c, x)
            for t in range(2):
                put(c * 32 + (x % 4) * 8, ((x // 4) * 2 + t) * 128, blocker.forward(v[8 * t : 8 * t + 8]))


def fine_smooth(blocker, columns, high, low, layer, put, finish=lambda bx: None):
    for bx in range(2):
        half = slice(bx * 256, bx * 256 + 256)
        total = block_product(columns[:, half], high, low, layer[:, half]) * damping
        for c in range(6):
            for x in range(4):
                row = c * 32 + x * 8
                for t in range(2):
                    put(c, 4 * bx + x, t, blocker.inverse(total[row : row + 8, 128 * t : 128 * t + 128]))
        finish(bx)


def store_columns(columns):
    def put(row, lane, v):
        columns[row : row + 8, lane : lane + 128] = v

    return put


def coarse_smooth(blocker, columns, get, high, low, layer):
    for c in range(6):
        for x in range(4):
            row = c * 32 + x * 8
            columns[row : row + 8, :] = blocker.forward(get(c, x))
    x = columns[...]
    x_high = x.astype(BF16)
    x_low = (x - x_high.astype(F32)).astype(BF16)
    both = jnp.where(lane_of(x.shape) < 64, x_high.astype(F32), x_low.astype(F32)).astype(BF16)
    total = jnp.zeros(x.shape, F32)
    for index in range(high.shape[0]):
        part = dot(high[index], both) + dot(low[index], both)
        total = jnp.where(layer == index, part, total)
    total = (total + pltpu.roll(total, 64, 1)) * (damping * 4.0)
    return lambda c, x: blocker.inverse(total[c * 32 + x * 8 : c * 32 + x * 8 + 8])


def first_kernel(
    source_hbm, depth_hbm, inverses_hbm, conductivity_hbm, x0, b0, high, low, layers, table, x_far, x_near, y_far, y_near,
    source, depth, inverses, conductivity, columns, done,
):
    copies = [
        pltpu.make_async_copy(source_hbm, source, done.at[0]),
        pltpu.make_async_copy(depth_hbm, depth, done.at[1]),
        pltpu.make_async_copy(inverses_hbm, inverses, done.at[2]),
        pltpu.make_async_copy(conductivity_hbm, conductivity, done.at[3]),
    ]
    for copy in copies:
        copy.start()
    blocker = Blocker(64)
    split = split_index((16, 128))
    copies[0].wait()

    for c in range(6):
        for x in range(8):
            b0[c, x] = take_lanes(source[c, x], split)
    fine_columns(blocker, lambda c, x: b0[c, x], store_columns(columns))
    copies[1].wait()
    layers[0:1, :] = fine_layers(depth)
    layers[1:2, 0:128] = coarse_layers(depth)
    copies[3].wait()
    values = jnp.broadcast_to(conductivity[...], (8, 8))
    own = jnp.where(row_of((8, 8)) == lane_of((8, 8)), values, 0.0)
    table[...] = jnp.broadcast_to(jnp.sum(own, axis=1, keepdims=True), (8, 128))
    copies[2].wait()
    for index in range(8):
        m = inverses[index]
        m_high = m.astype(BF16)
        high[index] = m_high
        low[index] = (m - m_high.astype(F32)).astype(BF16)

    def put(c, x, t, v):
        x0[c, x, 8 * t : 8 * t + 8, :] = v

    fine_smooth(blocker, columns, high, low, layers[0:1, :], put)
    for c in range(6):
        x_near[c], x_far[c] = near_far("gx", x0[c, 0], x0[c, 7])
        y_near[c, 0:8], y_far[c, 0:8] = near_far("gy", x0[c, :, 0, :], x0[c, :, 15, :])
        y_near[c, 8:16] = y_near[c, 0:8]
        y_far[c, 8:16] = y_far[c, 0:8]


def around(u, y_before, y_after, half, other, keep, row):
    size = u.shape[0]
    before = jnp.where(row == 0, y_before, pltpu.roll(u, 1, 0))
    after = jnp.where(row == size - 1, y_after, pltpu.roll(u, size - 1, 0))
    return before + after + pltpu.roll(u, half, 1) + jnp.where(keep, take_lanes(u, other), 0.0)


def fine_other(shape):
    j = lane_of(shape)
    return jnp.where(j < 64, jnp.maximum(j + 63, 64), jnp.minimum(j - 63, 63)), (j != 0) & (j != 127)


def coarse_other(shape):
    j = lane_of(shape) & 63
    return jnp.where(j < 32, jnp.maximum(j + 31, 32), jnp.minimum(j - 31, 31)), (j != 0) & (j != 63)


def pair_index(shape):
    j = lane_of(shape)
    return ((j & 31) << 1) | ((j >> 5) & 1)


def own_kernel(classes, table, b0, x0, r0, b1, sigma0, sigma1, rows, sums):
    shape = (16, 128)
    split = split_index(shape)
    other, keep = fine_other(shape)
    row = row_of(shape)
    pair = pair_index(shape)

    for x in range(8):
        kind = take_lanes(classes[x], split)
        sigma = jnp.zeros(shape, F32)
        for index in range(8):
            sigma = jnp.where(kind == index, table[index : index + 1, :], sigma)
        sigma0[x] = sigma
    for xx in range(4):
        sums[xx * 7 + 6] = sigma0[2 * xx] + sigma0[2 * xx + 1]
        for c in range(3):
            total = {}
            for x in (2 * xx, 2 * xx + 1):
                re = x0[c, x]
                im = x0[c + 3, x]
                sigma = sigma0[x]
                for comp, u, turn in ((c, re, -im), (c + 3, im, re)):
                    beside = around(u, 0.0, 0.0, 64, other, keep, row)
                    if x > 0:
                        beside = beside + x0[comp, x - 1]
                    if x < 7:
                        beside = beside + x0[comp, x + 1]
                    rest = b0[comp, x] - (6.0 * u - beside + sigma * turn)
                    r0[comp, x] = rest
                    total[comp] = rest + total[comp] if comp in total else rest
            for comp in total:
                sums[xx * 7 + comp] = total[comp]
    for slot in range(28):
        v = sums[slot]
        rows[slot] = take_lanes(v + pltpu.roll(v, 64, 1), pair)
    for xx in range(4):
        for c in range(7):
            slot = xx * 7 + c
            v = (rows[slot, pl.ds(0, 8, stride=2), :] + rows[slot, pl.ds(1, 8, stride=2), :]) * 0.125
            if c < 6:
                b1[c, xx] = v
            else:
                sigma1[xx] = v


def second_kernel(
    own_b1, edges, layers, x_far_in, x_near_in, y_far_in, y_near_in, high, low,
    b1, x1, x_far, x_near, y_far, y_near, rows, columns,
):
    shape = (16, 128)
    pair = pair_index(shape)
    narrow = (8, 128)
    row = row_of(narrow)
    for c in range(6):
        added = []
        for side, v in enumerate(before_after("gx", x_near_in[c], x_far_in[c])):
            slot = 2 * c + side
            rows[slot] = take_lanes(v + pltpu.roll(v, 64, 1), pair)
            added.append((rows[slot, pl.ds(0, 8, stride=2), :] + rows[slot, pl.ds(1, 8, stride=2), :]) * 0.125)
        edges = []
        for v in before_after("gy", y_near_in[c, 0:8], y_far_in[c, 0:8]):
            v = take_lanes(v + pltpu.roll(v, 64, 1), pair[0:8])
            edges.append((v + pltpu.roll(v, 7, 0)) * 0.125)
        for x in range(4):
            v = own_b1[c, x] + jnp.where(row == 0, edges[0][2 * x : 2 * x + 1], 0.0)
            v = v + jnp.where(row == 7, edges[1][2 * x : 2 * x + 1], 0.0)
            if x == 0:
                v = v + added[0]
            if x == 3:
                v = v + added[1]
            b1[c, x] = v
    result = coarse_smooth(Blocker(32), columns, lambda c, x: b1[c, x], high, low, layers[1:2, 0:128])
    store_coarse(result, x1, x_far, x_near, y_far, y_near)


def store_coarse(result, x1, x_far, x_near, y_far, y_near):
    for c in range(6):
        for x in range(4):
            x1[c, x] = result(c, x)
        x_near[c], x_far[c] = near_far("gx", x1[c, 0], x1[c, 3])
        y_near[c, 0:4], y_far[c, 0:4] = near_far("gy", x1[c, :, 0, :], x1[c, :, 7, :])
        y_near[c, 4:8] = y_near[c, 0:4]
        y_far[c, 4:8] = y_far[c, 0:4]


def middle_kernel(layers, x0, r0, x_far_in, x_near_in, y_far_in, y_near_in, high, low, y0, columns):
    blocker = Blocker(64)
    row = row_of((16, 128))
    x_halo = [before_after("gx", x_near_in[c], x_far_in[c]) for c in range(6)]
    y_halo = [before_after("gy", y_near_in[c, 0:8], y_far_in[c, 0:8]) for c in range(6)]

    def get(c, x):
        v = r0[c, x] + jnp.where(row == 0, y_halo[c][0][x : x + 1], 0.0)
        v = v + jnp.where(row == 15, y_halo[c][1][x : x + 1], 0.0)
        if x == 0:
            v = v + x_halo[c][0]
        if x == 7:
            v = v + x_halo[c][1]
        return v

    fine_columns(blocker, get, store_columns(columns))

    def put(c, x, t, v):
        y0[c, x, 8 * t : 8 * t + 8, :] = x0[c, x, 8 * t : 8 * t + 8, :] + v

    fine_smooth(blocker, columns, high, low, layers[0:1, :], put)


def third_kernel(
    layers, y0, b1, x1a, sigma1, x_far_in, x_near_in, y_far_in, y_near_in, high, low,
    x1, x_far, x_near, y_far, y_near, columns,
):
    x_halo = [before_after("gx", x_near_in[c], x_far_in[c]) for c in range(6)]
    y_halo = [before_after("gy", y_near_in[c], y_far_in[c]) for c in range(6)]
    shape = (8, 128)
    other, keep = coarse_other(shape)
    row = row_of(shape)

    def residual(c, x):
        u = x1a[c, x]
        turn = -x1a[c + 3, x] if c < 3 else x1a[c - 3, x]
        beside = around(u, y_halo[c][0][x : x + 1], y_halo[c][1][x : x + 1], 32, other, keep, row)
        beside = beside + (x1a[c, x - 1] if x > 0 else x_halo[c][0])
        beside = beside + (x1a[c, x + 1] if x < 3 else x_halo[c][1])
        return b1[c, x] - ((6.0 * u - beside) * 0.25 + sigma1[x] * turn)

    more = coarse_smooth(Blocker(32), columns, residual, high, low, layers[1:2, 0:128])
    store_coarse(lambda c, x: x1a[c, x] + more(c, x), x1, x_far, x_near, y_far, y_near)


def self_index(shape):
    k = lane_of(shape) & 63
    return ((k & 1) << 5) | (k >> 1)


def prolong_kernel(x1, sigma0, y0, layers, high, low, base, image, coarse, rows, columns):
    shape = (8, 128)
    j = lane_of(shape)
    row = row_of(shape)
    k = j & 63
    beyond = jnp.where(j < 64, k - 1, k + 1)
    inside = (beyond >= 0) & (beyond < 64)
    beyond = jnp.clip(beyond, 0, 63)
    next_index = ((beyond & 1) << 5) | (beyond >> 1)
    own_index = self_index(shape)

    for c in range(6):
        for x in range(4):
            coarse[c, x] = take_lanes(x1[c, x], own_index)
    for xx in range(4):
        for c in range(3):
            own = {}
            for comp in (c, c + 3):
                v = coarse[comp, xx]
                beside = jnp.where(inside, take_lanes(x1[comp, xx], next_index), 0.0)
                before = jnp.where(row == 0, 0.0, pltpu.roll(v, 1, 0))
                after = jnp.where(row == 7, 0.0, pltpu.roll(v, 7, 0))
                own[comp] = (v, 3.0 * v - beside, before, after)
                rows[comp, xx, pl.ds(0, 8, stride=2), :] = v
                rows[comp, xx, pl.ds(1, 8, stride=2), :] = v
            for half in range(2):
                x = 2 * xx + half
                next_x = xx - 1 + 2 * half
                for parity in range(2):
                    sigma = sigma0[x, pl.ds(parity, 8, stride=2), :]
                    for comp, partner, sign in ((c, c + 3, -1.0), (c + 3, c, 1.0)):
                        v, kept, before, after = own[comp]
                        value = kept - (before, after)[parity] + sign * sigma * own[partner][0]
                        if 0 <= next_x < 4:
                            value = value - coarse[comp, next_x]
                        image[comp, x, pl.ds(parity, 8, stride=2), :] = value
                for comp in (c, c + 3):
                    base[comp, x] = y0[comp, x] + rows[comp, xx]

    blocker = Blocker(64)
    fine_columns(blocker, lambda c, x: image[c, x], store_columns(columns))

    def put(c, x, t, v):
        part = slice(8 * t, 8 * t + 8)
        base[c, x, part, :] = base[c, x, part, :] - v

    fine_smooth(blocker, columns, high, low, layers[0:1, :], put)


FACES = 36


def edge_kernel(high, low, edges):
    i = row_of((192, 128))
    n = lane_of((192, 128))
    n = n - jnp.where(n >= FACES, FACES, 0) - jnp.where(n >= 2 * FACES, FACES, 0)
    face = jnp.where(n >= 12, 1, 0) + jnp.where(n >= 24, 1, 0)
    n = n - 12 * face
    x = (i >> 3) & 3
    y = (i >> 1) & 3
    same = ((i >> 5) == (n >> 1)) & (n < 12)
    lane = lane_of((192, 128))
    middle = (lane >= FACES) & (lane < 2 * FACES)
    for bx in range(2):
        on_x = (face == 0) & (x == 3 * bx) & ((y >> 1) == (n & 1))
        on_first = (face == 1) & (y == 0) & ((x >> 1) == (n & 1))
        on_last = (face == 2) & (y == 3) & ((x >> 1) == (n & 1))
        sums = jnp.where(same & (on_x | on_first | on_last), 1.0, 0.0).astype(BF16)
        for index in range(8):
            v = dot(high[index], sums) + dot(low[index], sums)
            v_high = v.astype(BF16).astype(F32)
            edges[bx * 8 + index] = jnp.where(middle, v - v_high, v_high).astype(BF16)


def last_kernel(layers, base, x_far_in, x_near_in, y_far_in, y_near_in, edges, out, stage, values, done):
    shape = (8, 128)
    own_index = self_index(shape)
    first_half = lane_of((1, 128)) < 64
    zero = jnp.zeros((1, 128), F32)
    for bx in range(2):
        values[bx, FACES:128] = jnp.zeros((128 - FACES, 256), F32)
    for c in range(6):
        x_faces = [take_lanes(v, own_index) for v in before_after("gx", x_near_in[c], x_far_in[c])]
        y_faces = [take_lanes(v, own_index) for v in before_after("gy", y_near_in[c], y_far_in[c])]
        for bx in range(2):
            v = x_faces[bx]
            for q in range(2):
                row = c * 2 + q
                x = 2 * bx + q
                for t in range(2):
                    y = 4 * t + q
                    values[bx, row : row + 1, 128 * t : 128 * t + 128] = jnp.where(
                        first_half, v[y : y + 1], v[y + 2 : y + 3]
                    )
                values[bx, 12 + row : 13 + row, 0:128] = jnp.where(first_half, y_faces[0][x : x + 1], 0.0)
                values[bx, 12 + row : 13 + row, 128:256] = zero
                values[bx, 24 + row : 25 + row, 0:128] = zero
                values[bx, 24 + row : 25 + row, 128:256] = jnp.where(first_half, 0.0, y_faces[1][x : x + 1])
    blocker = Blocker(64)
    join = join_index((16, 128))
    copies = []
    for bx in range(2):
        v = values[bx]
        v_high = v.astype(BF16).astype(F32)
        values[bx, FACES : 2 * FACES] = v_high[0:FACES]
        values[bx, 2 * FACES : 3 * FACES] = (v - v_high)[0:FACES]
        columns = values[bx].astype(BF16)
        total = jnp.zeros((192, 256), F32)
        for index in range(8):
            total = jnp.where(layers[0:1, 0:256] == index, dot(edges[bx * 8 + index], columns), total)
        total = total * damping
        for c in range(6):
            for x in range(4):
                row = c * 32 + x * 8
                for t in range(2):
                    part = slice(8 * t, 8 * t + 8)
                    v = blocker.inverse(total[row : row + 8, 128 * t : 128 * t + 128])
                    stage[c, 4 * bx + x, part, :] = base[c, 4 * bx + x, part, :] + v
        for c in range(6):
            for x in range(4 * bx, 4 * bx + 4):
                stage[c, x] = take_lanes(stage[c, x], join)
        part = pl.ds(4 * bx, 4)
        copies.append(pltpu.make_async_copy(stage.at[:, part], out.at[:, part], done.at[bx]))
        copies[bx].start()
    for copy in copies:
        copy.wait()


def call(kernel, outs, args, scratch, spaces=(), last=False):
    vmem = pl.BlockSpec(memory_space=pltpu.VMEM)
    own = len(spaces)
    args = [pltpu.with_memory_space_constraint(arg, space) for arg, space in zip(args, spaces)] + [pltpu.with_memory_space_constraint(arg, pltpu.VMEM) for arg in args[own:]]
    return pl.pallas_call(
        kernel,
        out_shape=[jax.ShapeDtypeStruct(*out) if last else pltpu.VMEM(*out) for out in outs],
        in_specs=[pl.BlockSpec(memory_space=space) for space in spaces] + [vmem] * (len(args) - own),
        out_specs=[pl.BlockSpec(memory_space=pltpu.HBM) if last else vmem] * len(outs),
        scratch_shapes=scratch,
        compiler_params=pltpu.CompilerParams(vmem_limit_bytes=12 << 20),
        name=kernel.__name__,
    )(*args)


def exchange(x_far, x_near, y_far, y_near):
    nx, ny = lax.axis_size("gx"), lax.axis_size("gy")

    def swapped(array, partner):
        pairs = [(i * ny + j, partner(i, j)) for i in range(nx) for j in range(ny)]
        return lax.ppermute(array, ("gx", "gy"), [(a, i * ny + j) for a, (i, j) in pairs])

    def far(i):
        return i + 1 if i % 2 else i - 1

    def x_far_partner(i, j):
        return (i, j ^ 1) if i in (0, nx - 1) else (far(i), j)

    def y_far_partner(i, j):
        return (i ^ 1, j) if j in (0, ny - 1) else (i, far(j))

    return (
        swapped(x_far, x_far_partner),
        swapped(x_near, lambda i, j: (i ^ 1, j)),
        swapped(y_far, y_far_partner),
        swapped(y_near, lambda i, j: (i, j ^ 1)),
    )


def near_far(axis, first, last):
    even = lax.axis_index(axis) % 2 == 0
    return jnp.where(even, last, first), jnp.where(even, first, last)


def before_after(axis, near, far):
    place = lax.axis_index(axis)
    even = place % 2 == 0
    before = jnp.where(place > 0, jnp.where(even, far, near), 0.0)
    after = jnp.where(place < lax.axis_size(axis) - 1, jnp.where(even, near, far), 0.0)
    return before, after


def per_device(source, cell_class, class_conductivity, layer_of_depth, inverses):
    fine = ((6, 8, 16, 128), F32)
    coarse = ((6, 4, 8, 128), F32)
    matrices = ((8, 192, 192), BF16)
    fine_faces = [((6, 16, 128), F32)] * 4
    coarse_faces = [((6, 8, 128), F32)] * 4
    columns = pltpu.VMEM((192, 512), F32)
    coarse_columns = pltpu.VMEM((192, 128), F32)

    x0, b0, high, low, layers, table, *faces = call(
        first_kernel,
        [fine, fine, matrices, matrices, ((8, 512), jnp.int32), ((8, 128), F32)] + fine_faces,
        (source, layer_of_depth.reshape(1, 64), inverses, class_conductivity.reshape(1, 8)),
        [
            pltpu.VMEM(source.shape, F32),
            pltpu.VMEM((1, 64), jnp.int32),
            pltpu.VMEM(inverses.shape, F32),
            pltpu.VMEM((1, 8), F32),
            columns,
            pltpu.SemaphoreType.DMA((4,)),
        ],
        spaces=(pltpu.HBM,) * 4,
    )
    halos = exchange(*faces)
    r0, own_b1, sigma0, sigma1 = call(
        own_kernel,
        [fine, coarse, ((8, 16, 128), F32), ((4, 8, 128), F32)],
        (cell_class, table, b0, x0),
        [pltpu.VMEM((28, 16, 128), F32)] * 2,
        spaces=(pltpu.VMEM,),
    )
    (edges,) = call(edge_kernel, [((16, 192, 128), BF16)], (high, low), [])
    b1, x1a, *faces = call(
        second_kernel,
        [coarse, coarse] + coarse_faces,
        (own_b1, edges, layers, *halos, high, low),
        [pltpu.VMEM((12, 16, 128), F32), coarse_columns],
    )
    fine_halos = halos
    halos = exchange(*faces)
    (y0,) = call(middle_kernel, [fine], (layers, x0, r0, *fine_halos, high, low), [columns])
    x1, *faces = call(
        third_kernel, [coarse] + coarse_faces, (layers, y0, b1, x1a, sigma1, *halos, high, low), [coarse_columns]
    )
    halos = exchange(*faces)
    (base,) = call(
        prolong_kernel,
        [fine],
        (x1, sigma0, y0, layers, high, low),
        [pltpu.VMEM(*fine), pltpu.VMEM((6, 4, 8, 128), F32), pltpu.VMEM((6, 4, 16, 128), F32), columns],
    )
    (out,) = call(
        last_kernel,
        [fine],
        (layers, base, *halos, edges),
        [pltpu.VMEM(*fine), pltpu.VMEM((2, 128, 256), F32), pltpu.SemaphoreType.DMA((2,))],
        last=True,
    )
    return out


def solution(mesh):
    placed = (P(None, "gx", "gy", None), P("gx", "gy", None), P(), P(), P())
    return jax.shard_map(
        per_device, mesh=mesh, in_specs=placed, out_specs=P(None, "gx", "gy", None), check_vma=False
    )
```
